512 devices in a mesh: dp: 32 (over x, z), tensor: 16 (over y, core).
Axes of the slice: x: 4, y: 8, z: 8, core: 2. Of those that a mesh axis runs over, the one named last changes fastest.
Arguments:
- activations: bfloat16 [8192, 4096], P('dp'), may hold values from -6 to 6
- grad_output: bfloat16 [8192, 14336], P('dp', 'tensor'), may hold values from -6 to 6
- weight: bfloat16 [4096, 14336], P('dp', 'tensor'), may hold values from -0.09375 to 0.09375
- start_basis: float32 [14336, 64], P('tensor'), may hold values from -6 to 6
Outputs:
- input_grad: bfloat16 [8192, 4096], P('dp', 'tensor')
- right_basis: float32 [14336, 64], P('tensor')
- new_weight: float32 [4096, 14336], P('dp', 'tensor')
The draws below stay inside these ranges and needn't reach their ends.
All inputs are finite; a program needn't handle non-finite values.
Results may differ from the reference program's by a relative error of at most 0.018.
Values may be sent and summed in bfloat16 or wider, within the bound.
No kernel may reach another device: no remote copies, remote signals or barrier semaphores. Data moves between devices by JAX's collectives and lax.ppermute only.
A program may use at most 128 MiB of HBM per device.

```python
import jax
import jax.numpy as jnp
from jax import lax

D = 4096
FF = 14336
RANK = 64
TOKENS = 8192
N_TENSOR = 16


def steps_of(own_key, extent, split, low, high):
    factor_of, own = 1.0, jax.random.fold_in(own_key, 6)
    for position, parts in split:
        draws = jnp.exp(jax.random.uniform(jax.random.fold_in(own, position), (parts,), jnp.float32, low / len(split), high / len(split)))
        factor_of = factor_of * jnp.repeat(draws, extent[position] // parts).reshape([-1 if axis == position else 1 for axis in range(len(extent))])
    return factor_of


def noise(stream_key, dims, spread, limit, shards=(), held_as=jnp.bfloat16):
    level = steps_of(stream_key, dims, shards, -0.22, 0.18) if shards else 1.0
    entries = jax.random.normal(stream_key, dims, jnp.float32) * spread * level
    return jnp.minimum(jnp.maximum(entries, -limit), limit).astype(held_as)


def setup_inputs(seed: int = 0) -> dict:
    streams_of = jax.random.split(jax.random.key(seed), 5)
    activations = noise(streams_of[0], (TOKENS, D), 1.0, 6.0, ((0, 32),))
    grad_output = noise(streams_of[1], (TOKENS, FF), 1.0, 6.0, ((0, 32), (1, 16)))
    weight = noise(streams_of[2], (D, FF), D ** -0.5, 0.09375, ((0, 32), (1, 16)))
    start_basis = noise(streams_of[3], (FF, RANK), 1.0, 6.0, ((0, 16),), jnp.float32)
    return {"activations": activations, "grad_output": grad_output, "weight": weight, "start_basis": start_basis}


learn_rate = 0.001

def reference(activations, grad_output, weight, start_basis):
    block_width = FF // N_TENSOR
    grad_blocks = grad_output.reshape(TOKENS, N_TENSOR, block_width).transpose(1, 0, 2)
    weight_blocks = weight.reshape(D, N_TENSOR, block_width).transpose(1, 0, 2)

    def add_block(total, pair):
        grad_piece, weight_piece = pair
        partial_sum = lax.dot_general(grad_piece.astype(jnp.float32), weight_piece.astype(jnp.float32), (((1,), (1,)), ((), ())), preferred_element_type=jnp.float32)
        return (total + partial_sum.astype(jnp.bfloat16).astype(jnp.float32), None)
    summed, _ = lax.scan(add_block, jnp.zeros((TOKENS, D), jnp.float32), (grad_blocks, weight_blocks))
    input_grad = summed.astype(jnp.bfloat16)
    gradient = lax.dot_general(activations.astype(jnp.float32), grad_output.astype(jnp.float32), (((0,), (0,)), ((), ())), preferred_element_type=jnp.float32)
    left = jnp.dot(gradient, start_basis, precision=lax.Precision.HIGHEST)
    gram_matrix = jnp.dot(left.T, left, precision=lax.Precision.HIGHEST)
    lower = jnp.linalg.cholesky(gram_matrix)
    left_basis = jax.scipy.linalg.solve_triangular(lower, left.T, lower=True).T
    right = jnp.dot(gradient.T, left_basis, precision=lax.Precision.HIGHEST)
    right_basis = right / jnp.sqrt(jnp.float32(TOKENS))
    update = jnp.dot(left_basis, right.T, precision=lax.Precision.HIGHEST)
    new_weight = weight.astype(jnp.float32) - learn_rate * update
    return (input_grad, right_basis, new_weight)
```

```python
import jax
import jax.numpy as jnp
from jax import lax
from jax.sharding import Mesh
from jax.sharding import PartitionSpec as P

DP = ("x", "z")
TENSOR = ("y", "c")
HIGH = lax.Precision.HIGHEST

learn_rate = 0.001


def swap(parts, axis):
    return lax.all_to_all(parts, axis, split_axis=0, concat_axis=0, tiled=True)


def share(x, axis):
    return swap(jnp.broadcast_to(x[None], (lax.axis_size(axis), *x.shape)), axis)


def input_gradient(grad_output, weight):
    n_x, n_z, n_y = (lax.axis_size(a) for a in ("x", "z", "y"))
    rows, hidden = weight.shape
    tokens = grad_output.shape[0]
    half = rows // 2
    halves = swap(weight.reshape(2, half, hidden), "c")
    weights = share(halves, "z")
    grads = share(grad_output, ("x", "c")).reshape(n_x, 2, tokens, hidden)
    weights = weights.reshape(2, n_z // 2, 2, half, hidden)
    partial = jnp.einsum("xkth,gzkrh->xgtzr", grads, weights, preferred_element_type=jnp.float32)
    parts = partial.astype(jnp.bfloat16).reshape(n_y, tokens, n_z // 2 * half)
    arrived = swap(parts, "y")
    summed = arrived.astype(jnp.float32).sum(axis=0).astype(jnp.bfloat16)
    pair = summed.reshape(tokens, 2, n_z // 4, half)
    core = lax.axis_index("c")
    flip = core == 1
    keep = jnp.where(flip, pair[:, 1], pair[:, 0])
    give = jnp.where(flip, pair[:, 0], pair[:, 1])
    keep_to, give_to = [], []
    for x in range(n_x):
        for y in range(n_y):
            for c in range(2):
                here = (x * n_y + y) * 2 + c
                there = ((y // 2) * n_y + 2 * x + y % 2) * 2
                keep_to.append((here, there + c))
                give_to.append((here, there + 1 - c))
    axes = ("x", "y", "c")
    mine = lax.ppermute(keep, axes, keep_to)
    other = lax.ppermute(give, axes, give_to)
    first = jnp.where(flip, other, mine)
    second = jnp.where(flip, mine, other)
    return jnp.stack([first, second], axis=2).reshape(tokens, -1)


def body(activations, grad_output, weight, start_basis):
    n_d, n_t = lax.axis_size(DP), lax.axis_size(TENSOR)
    tokens, features = activations.shape
    hidden = grad_output.shape[1]
    rows = weight.shape[0]
    rank = start_basis.shape[1]
    few = rank // n_t
    f32 = jnp.float32
    input_grad = input_gradient(grad_output, weight)
    a32, g32 = activations.astype(f32), grad_output.astype(f32)
    mixed = lax.dot_general(start_basis, g32, (((0,), (1,)), ((), ())), precision=HIGH)
    mixed = swap(mixed.reshape(n_t, few, tokens), TENSOR).sum(axis=0)
    left_part = jnp.dot(mixed, a32, precision=HIGH)
    left_part = jnp.swapaxes(left_part.reshape(few, n_d, rows), 0, 1)
    left_mine = swap(left_part, DP).sum(axis=0)
    left_few = jnp.swapaxes(share(left_mine, DP), 0, 1).reshape(few, features)
    seen = lax.dot_general(left_few, a32, (((1,), (1,)), ((), ())), precision=HIGH)
    both = share(jnp.concatenate([seen, left_mine], axis=1), TENSOR).reshape(rank, tokens + rows)
    seen, left_rows = both[:, :tokens], both[:, tokens:]
    right_part = jnp.dot(seen, g32, precision=HIGH)
    gram_part = lax.dot_general(left_rows, left_rows, (((1,), (1,)), ((), ())), precision=HIGH)
    pad = jnp.zeros((rank, 128 - rank), f32)
    packed = jnp.concatenate([right_part, gram_part, pad], axis=1).reshape(n_d, rank // n_d, -1)
    packed = share(swap(packed, DP).sum(axis=0), DP).reshape(rank, -1)
    right, gram_matrix = packed[:, :hidden], packed[:, hidden : hidden + rank]
    lower = jnp.linalg.cholesky(gram_matrix)
    solved = jax.scipy.linalg.solve_triangular(
        lower, jnp.concatenate([right, left_rows], axis=1), lower=True
    )
    right, basis_rows = solved[:, :hidden], solved[:, hidden:]
    right_basis = right.T / jnp.sqrt(f32(tokens * n_d))
    update = lax.dot_general(basis_rows, right, (((0,), (0,)), ((), ())), precision=HIGH)
    new_weight = weight.astype(f32) - learn_rate * update
    return (input_grad, right_basis, new_weight)


def solution(mesh):
    finer = Mesh(mesh.devices.reshape(4, 8, 8, 2), ("x", "z", "y", "c"))
    in_specs = (P(DP, None), P(DP, TENSOR), P(DP, TENSOR), P(TENSOR, None))
    out_specs = (P(DP, TENSOR), P(TENSOR, None), P(DP, TENSOR))
    return jax.shard_map(body, mesh=finer, in_specs=in_specs, out_specs=out_specs, check_vma=False)
```

```python
import functools

import jax
import jax.numpy as jnp
from jax import lax
from jax.experimental import pallas as pl
from jax.experimental.pallas import tpu as pltpu
from jax.sharding import Mesh
from jax.sharding import PartitionSpec as P


DP = ("x", "z")
TENSOR = ("y", "c")
HIGH = lax.Precision.HIGHEST

learn_rate = 0.001


def swap(parts, axis):
    return lax.all_to_all(parts, axis, split_axis=0, concat_axis=0, tiled=True)


def share(x, axis):
    return swap(jnp.broadcast_to(x[None], (lax.axis_size(axis), *x.shape)), axis)


def shifted(x, axis, by):
    length = lax.axis_size(axis)
    return lax.ppermute(x, axis, [(i, (i + by) % length) for i in range(length)])


def block_kernel(n_x, n_z, n_y, where, *refs):
    grads, weights = refs[:n_x], refs[n_x : n_x + n_z]
    outs = refs[n_x + n_z : n_x + n_z + n_y]
    packed, parts = refs[n_x + n_z + n_y :]
    x, z, y = where[0], where[1], where[2]
    half, hidden = weights[0].shape[1:]
    group = n_z // 2
    for s in range(n_z):
        packed[lax.rem(z - s + n_z, n_z)] = weights[s][...]
    dims = (((1,), (1,)), ((), ()))
    for h in range(2):
        rows = packed[h * group : (h + 1) * group]
        first = rows[:, 0].reshape(group * half, hidden)
        second = rows[:, 1].reshape(group * half, hidden)
        for s in range(n_x):
            total = lax.dot_general(grads[s][0], first, dims, preferred_element_type=jnp.float32)
            total += lax.dot_general(grads[s][1], second, dims, preferred_element_type=jnp.float32)
            parts[2 * lax.rem(x - s + n_x, n_x) + h] = total.astype(jnp.bfloat16)
    for s in range(n_y):
        outs[s][...] = parts[lax.rem(y + s, n_y)]


def input_gradient(grad_output, weight):
    n_x, n_z, n_y = (lax.axis_size(a) for a in ("x", "z", "y"))
    rows, hidden = weight.shape
    tokens = grad_output.shape[0]
    half = rows // 2
    core = lax.axis_index("c")
    flip = core == 1
    keep = jnp.where(flip, weight[half:], weight[:half])
    give = jnp.where(flip, weight[:half], weight[half:])
    weights = jnp.stack([keep, shifted(give, "c", 1)])
    grads = jnp.stack([grad_output, shifted(grad_output, "c", 1)])
    weights = [weights] + [shifted(weights, "z", s) for s in range(1, n_z)]
    grads = [grads] + [shifted(grads, "x", s) for s in range(1, n_x)]
    where = jnp.stack([lax.axis_index(a) for a in ("x", "z", "y")]).astype(jnp.int32)
    width = n_z // 2 * half
    vmem = pl.BlockSpec(memory_space=pltpu.VMEM)
    parts = pl.pallas_call(
        functools.partial(block_kernel, n_x, n_z, n_y),
        out_shape=[jax.ShapeDtypeStruct((tokens, width), jnp.bfloat16)] * n_y,
        in_specs=[pl.BlockSpec(memory_space=pltpu.SMEM)] + [vmem] * (n_x + n_z),
        out_specs=[vmem] * n_y,
        scratch_shapes=[
            pltpu.VMEM((n_z, 2, half, hidden), jnp.bfloat16),
            pltpu.VMEM((n_y, tokens, width), jnp.bfloat16),
        ],
        name="blocks",
    )(where, *grads, *weights)
    arrived = [parts[0]] + [shifted(parts[s], "y", s) for s in range(1, n_y)]
    summed = sum(a.astype(jnp.float32) for a in arrived).astype(jnp.bfloat16)
    pair = summed.reshape(tokens, 2, n_z // 4, half)
    keep = jnp.where(flip, pair[:, 1], pair[:, 0])
    give = jnp.where(flip, pair[:, 0], pair[:, 1])
    keep_to, give_to = [], []
    for x in range(n_x):
        for y in range(n_y):
            for c in range(2):
                here = (x * n_y + y) * 2 + c
                there = ((y // 2) * n_y + 2 * x + y % 2) * 2
                keep_to.append((here, there + c))
                give_to.append((here, there + 1 - c))
    axes = ("x", "y", "c")
    mine = lax.ppermute(keep, axes, keep_to)
    other = lax.ppermute(give, axes, give_to)
    first = jnp.where(flip, other, mine)
    second = jnp.where(flip, mine, other)
    return jnp.stack([first, second], axis=2).reshape(tokens, -1)


def step(activations, grad_output, weight, start_basis):
    n_d, n_t = lax.axis_size(DP), lax.axis_size(TENSOR)
    tokens, features = activations.shape
    hidden = grad_output.shape[1]
    rows = weight.shape[0]
    rank = start_basis.shape[1]
    few = rank // n_t
    f32 = jnp.float32
    input_grad = input_gradient(grad_output, weight)
    a32, g32 = activations.astype(f32), grad_output.astype(f32)
    mixed = lax.dot_general(start_basis, g32, (((0,), (1,)), ((), ())), precision=HIGH)
    mixed = swap(mixed.reshape(n_t, few, tokens), TENSOR)
    mixed = mixed.sum(axis=0)
    left_part = jnp.dot(mixed, a32, precision=HIGH)
    left_part = jnp.swapaxes(left_part.reshape(few, n_d, rows), 0, 1)
    left_mine = swap(left_part, DP)
    left_mine = left_mine.sum(axis=0)
    left_few = jnp.swapaxes(share(left_mine, DP), 0, 1).reshape(few, features)
    seen = lax.dot_general(left_few, a32, (((1,), (1,)), ((), ())), precision=HIGH)
    both = share(jnp.concatenate([seen, left_mine], axis=1), TENSOR).reshape(rank, tokens + rows)
    seen, left_rows = both[:, :tokens], both[:, tokens:]
    right_part = jnp.dot(seen, g32, precision=HIGH)
    gram_part = lax.dot_general(left_rows, left_rows, (((1,), (1,)), ((), ())), precision=HIGH)
    pad = jnp.zeros((rank, 128 - rank), f32)
    packed = jnp.concatenate([right_part, gram_part, pad], axis=1).reshape(n_d, rank // n_d, -1)
    packed = share(swap(packed, DP).sum(axis=0), DP).reshape(rank, -1)
    right, gram_matrix = packed[:, :hidden], packed[:, hidden : hidden + rank]
    lower = jnp.linalg.cholesky(gram_matrix)
    solved = jax.scipy.linalg.solve_triangular(
        lower, jnp.concatenate([right, left_rows], axis=1), lower=True
    )
    right, basis_rows = solved[:, :hidden], solved[:, hidden:]
    right_basis = right.T / jnp.sqrt(f32(tokens * n_d))
    update = lax.dot_general(basis_rows, right, (((0,), (0,)), ((), ())), precision=HIGH)
    new_weight = weight.astype(f32) - learn_rate * update
    return (input_grad, right_basis, new_weight)


def solution(mesh):
    finer = Mesh(mesh.devices.reshape(4, 8, 8, 2), ("x", "z", "y", "c"))
    in_specs = (P(DP, None), P(DP, TENSOR), P(DP, TENSOR), P(TENSOR, None))
    out_specs = (P(DP, TENSOR), P(TENSOR, None), P(DP, TENSOR))
    return jax.shard_map(step, mesh=finer, in_specs=in_specs, out_specs=out_specs, check_vma=False)
```

```python
import functools

import jax
import jax.numpy as jnp
from jax import lax
from jax.experimental import pallas as pl
from jax.experimental.pallas import tpu as pltpu
from jax.sharding import Mesh
from jax.sharding import PartitionSpec as P


DP = ("x", "z")
TENSOR = ("y", "c")
HIGH = lax.Precision.HIGHEST

learn_rate = 0.001


def swap(parts, axis):
    return lax.all_to_all(parts, axis, split_axis=0, concat_axis=0, tiled=True)


def share(x, axis):
    return swap(jnp.broadcast_to(x[None], (lax.axis_size(axis), *x.shape)), axis)


def shifted(x, axis, by):
    length = lax.axis_size(axis)
    return lax.ppermute(x, axis, [(i, (i + by) % length) for i in range(length)])


def block_kernel(n_x, where, *refs):
    grads, weights = refs[:n_x], refs[n_x]
    earlier, parts = refs[n_x + 1 : -1], refs[-1]
    x, side = where[0], where[1]
    _, rows, hidden = weights.shape
    dims = (((1,), (1,)), ((), ()))
    for h in range(2):
        block = weights[pl.ds(4 * h + 2 * side, 2)].reshape(2 * rows, hidden)
        for s in range(n_x):
            total = lax.dot_general(grads[s][...], block, dims, preferred_element_type=jnp.float32)
            place = 2 * lax.rem(x - s + n_x, n_x) + h
            if earlier:
                total += earlier[0][place].astype(jnp.float32)
            parts[place] = total.astype(jnp.bfloat16)


def block_products(side, grads, weights, earlier=()):
    n_x, n_y = lax.axis_size("x"), lax.axis_size("y")
    tokens, rows = grads[0].shape[0], weights.shape[1]
    vmem = pl.BlockSpec(memory_space=pltpu.VMEM)
    where = jnp.stack([lax.axis_index("x"), side]).astype(jnp.int32)
    return pl.pallas_call(
        functools.partial(block_kernel, n_x),
        out_shape=jax.ShapeDtypeStruct((n_y, tokens, 2 * rows), jnp.bfloat16),
        in_specs=[pl.BlockSpec(memory_space=pltpu.SMEM)] + [vmem] * (n_x + 1 + len(earlier)),
        out_specs=vmem,
        name="blocks",
    )(where, *grads, weights, *earlier)


def input_gradient(grad_output, weight):
    n_x, n_y = lax.axis_size("x"), lax.axis_size("y")
    core = lax.axis_index("c")
    weights = lax.all_gather(weight, "z", axis=0)
    grads = [grad_output] + [shifted(grad_output, "x", s) for s in range(1, n_x)]
    give = block_products(1 - core, grads, weights)
    arrived = shifted(give, "c", 1)
    parts = block_products(core, grads, weights, (arrived,))
    summed = lax.psum_scatter(parts, "y", scatter_dimension=0)
    to = []
    for x in range(n_x):
        for y in range(n_y):
            for c in range(2):
                to.append(((x * n_y + y) * 2 + c, ((y // 2) * n_y + 2 * x + y % 2) * 2 + c))
    return lax.ppermute(summed, ("x", "y", "c"), to)


def step(activations, grad_output, weight, start_basis):
    n_d, n_t = lax.axis_size(DP), lax.axis_size(TENSOR)
    tokens, features = activations.shape
    hidden = grad_output.shape[1]
    rows = weight.shape[0]
    rank = start_basis.shape[1]
    few = rank // n_t
    f32 = jnp.float32
    input_grad = input_gradient(grad_output, weight)
    a32, g32 = activations.astype(f32), grad_output.astype(f32)
    mixed = lax.dot_general(start_basis, g32, (((0,), (1,)), ((), ())), precision=HIGH)
    mixed = swap(mixed.reshape(n_t, few, tokens), TENSOR)
    mixed = mixed.sum(axis=0)
    left_part = jnp.dot(mixed, a32, precision=HIGH)
    left_part = jnp.swapaxes(left_part.reshape(few, n_d, rows), 0, 1)
    left_mine = swap(left_part, DP)
    left_mine = left_mine.sum(axis=0)
    left_few = jnp.swapaxes(share(left_mine, DP), 0, 1).reshape(few, features)
    seen = lax.dot_general(left_few, a32, (((1,), (1,)), ((), ())), precision=HIGH)
    both = share(jnp.concatenate([seen, left_mine], axis=1), TENSOR).reshape(rank, tokens + rows)
    seen, left_rows = both[:, :tokens], both[:, tokens:]
    right_part = jnp.dot(seen, g32, precision=HIGH)
    gram_part = lax.dot_general(left_rows, left_rows, (((1,), (1,)), ((), ())), precision=HIGH)
    pad = jnp.zeros((rank, 128 - rank), f32)
    packed = jnp.concatenate([right_part, gram_part, pad], axis=1).reshape(n_d, rank // n_d, -1)
    packed = share(swap(packed, DP).sum(axis=0), DP).reshape(rank, -1)
    right, gram_matrix = packed[:, :hidden], packed[:, hidden : hidden + rank]
    lower = jnp.linalg.cholesky(gram_matrix)
    solved = jax.scipy.linalg.solve_triangular(
        lower, jnp.concatenate([right, left_rows], axis=1), lower=True
    )
    right, basis_rows = solved[:, :hidden], solved[:, hidden:]
    right_basis = right.T / jnp.sqrt(f32(tokens * n_d))
    update = lax.dot_general(basis_rows, right, (((0,), (0,)), ((), ())), precision=HIGH)
    new_weight = weight.astype(f32) - learn_rate * update
    return (input_grad, right_basis, new_weight)


def solution(mesh):
    finer = Mesh(mesh.devices.reshape(4, 8, 8, 2), ("x", "z", "y", "c"))
    in_specs = (P(DP, None), P(DP, TENSOR), P(DP, TENSOR), P(TENSOR, None))
    out_specs = (P(DP, TENSOR), P(TENSOR, None), P(DP, TENSOR))
    return jax.shard_map(step, mesh=finer, in_specs=in_specs, out_specs=out_specs, check_vma=False)
```

```python
import functools

import jax
import jax.numpy as jnp
from jax import lax
from jax.experimental import pallas as pl
from jax.experimental.pallas import tpu as pltpu
from jax.sharding import Mesh
from jax.sharding import PartitionSpec as P


DP = ("x", "z")
TENSOR = ("y", "c")
HIGH = lax.Precision.HIGHEST

learn_rate = 0.001


def swap(parts, axis):
    return lax.all_to_all(parts, axis, split_axis=0, concat_axis=0, tiled=True)


def share(x, axis):
    return swap(jnp.broadcast_to(x[None], (lax.axis_size(axis), *x.shape)), axis)


def shifted(x, axis, by):
    length = lax.axis_size(axis)
    return lax.ppermute(x, axis, [(i, (i + by) % length) for i in range(length)])


def block_kernel(n_x, where, *refs):
    grads, weights = refs[:n_x], refs[n_x]
    earlier, parts = refs[n_x + 1 : -1], refs[-1]
    x, side = where[0], where[1]
    _, rows, hidden = weights.shape
    dims = (((1,), (1,)), ((), ()))
    for h in range(2):
        block = weights[pl.ds(4 * h + 2 * side, 2)].reshape(2 * rows, hidden)
        for s in range(n_x):
            total = lax.dot_general(grads[s][...], block, dims, preferred_element_type=jnp.float32)
            place = 2 * lax.rem(x - s + n_x, n_x) + h
            if earlier:
                total += earlier[0][place].astype(jnp.float32)
            parts[place] = total.astype(jnp.bfloat16)


def block_products(side, grads, weights, earlier=()):
    n_x, n_y = lax.axis_size("x"), lax.axis_size("y")
    tokens, rows = grads[0].shape[0], weights.shape[1]
    vmem = pl.BlockSpec(memory_space=pltpu.VMEM)
    where = jnp.stack([lax.axis_index("x"), side]).astype(jnp.int32)
    return pl.pallas_call(
        functools.partial(block_kernel, n_x),
        out_shape=jax.ShapeDtypeStruct((n_y, tokens, 2 * rows), jnp.bfloat16),
        in_specs=[pl.BlockSpec(memory_space=pltpu.SMEM)] + [vmem] * (n_x + 1 + len(earlier)),
        out_specs=vmem,
        name="blocks",
    )(where, *grads, weights, *earlier)


def input_gradient(grad_output, weight):
    n_x, n_y = lax.axis_size("x"), lax.axis_size("y")
    core = lax.axis_index("c")
    weights = lax.all_gather(weight, "z", axis=0)
    grads = [grad_output] + [shifted(grad_output, "x", s) for s in range(1, n_x)]
    give = block_products(1 - core, grads, weights)
    arrived = shifted(give, "c", 1)
    parts = block_products(core, grads, weights, (arrived,))
    summed = lax.psum_scatter(parts, "y", scatter_dimension=0)
    to = []
    for x in range(n_x):
        for y in range(n_y):
            for c in range(2):
                to.append(((x * n_y + y) * 2 + c, ((y // 2) * n_y + 2 * x + y % 2) * 2 + c))
    return lax.ppermute(summed, ("x", "y", "c"), to)


def thirds(value):
    first = value.astype(jnp.bfloat16)
    rest = value - first.astype(jnp.float32)
    second = rest.astype(jnp.bfloat16)
    third = (rest - second.astype(jnp.float32)).astype(jnp.bfloat16)
    return first, second, third


def exact_dot(value, other, dims):
    dot = functools.partial(lax.dot_general, dimension_numbers=(dims, ((), ())), preferred_element_type=jnp.float32)
    count = value.shape[0]
    parts = dot(jnp.concatenate(thirds(value), axis=0), other)
    return (parts[2 * count :] + parts[count : 2 * count]) + parts[:count]


def mixed_kernel(basis, grads, out):
    mixed = exact_dot(basis[...], grads[...], ((1,), (1,)))
    few = out.shape[1]
    for t in range(out.shape[0]):
        out[t] = mixed[t * few : (t + 1) * few]


def left_kernel(arrived, activations, out, lines):
    few = arrived.shape[1]
    mixed = arrived[0]
    for t in range(1, arrived.shape[0]):
        mixed += arrived[t]
    for i, part in enumerate(thirds(mixed)):
        lines[i * few : (i + 1) * few] = part.astype(jnp.float32)
    dot = jnp.dot(lines[: 3 * few].astype(jnp.bfloat16), activations[...], preferred_element_type=jnp.float32)
    total = (dot[2 * few :] + dot[few : 2 * few]) + dot[:few]
    rows = out.shape[2]
    for d in range(out.shape[0]):
        out[d] = total[:, d * rows : (d + 1) * rows]


def right_kernel(both, grads, out):
    tokens, hidden = grads.shape
    rank = both.shape[0]
    right = exact_dot(both[:, :tokens], grads[...], ((1,), (0,)))
    rows = both[:, tokens:]
    gram = lax.dot_general(rows, rows, (((1,), (1,)), ((), ())), precision=HIGH, preferred_element_type=jnp.float32)
    few = out.shape[1]
    for d in range(out.shape[0]):
        out[d, :, :hidden] = right[d * few : (d + 1) * few]
        out[d, :, hidden : hidden + rank] = gram[d * few : (d + 1) * few]
        out[d, :, hidden + rank :] = jnp.zeros((few, out.shape[2] - hidden - rank), jnp.float32)


def last_kernel(token_total, packed, left_rows, weight, right_basis, new_weight):
    rank = packed.shape[0]
    hidden = weight.shape[1]
    row = lax.broadcasted_iota(jnp.int32, (8, 2 * rank), 0)
    lane = lax.broadcasted_iota(jnp.int32, (8, 2 * rank), 1)
    blocks = []
    for j in range(rank // 8):
        gram = packed[8 * j : 8 * j + 8, hidden : hidden + 2 * rank]
        blocks.append(jnp.where(lane < rank, gram, jnp.where(lane - rank == row + 8 * j, 1.0, 0.0)))
    for k in range(rank):
        b, i = divmod(k, 8)
        pivot = blocks[b][i : i + 1]
        scaled = pivot / pivot[:, k : k + 1]
        for j in range(b, rank // 8):
            factor = blocks[j][:, k : k + 1]
            if j == b:
                factor = jnp.where(row[:, :1] > i, factor, 0.0)
            blocks[j] = blocks[j] - factor * scaled
    inverse = []
    for j, block in enumerate(blocks):
        pivots = jnp.sum(jnp.where(lane == row + 8 * j, block, 0.0), axis=1, keepdims=True)
        inverse.append(block / jnp.sqrt(pivots))
    inverse = jnp.concatenate(inverse, axis=0)[:, rank:]
    dot = functools.partial(jnp.dot, precision=HIGH, preferred_element_type=jnp.float32)
    right = dot(inverse, packed[:, :hidden])
    basis = dot(inverse, left_rows[...])
    right_basis[...] = right / jnp.sqrt(jnp.float32(token_total))
    new_weight[...] = weight[...].astype(jnp.float32) - learn_rate * dot(basis.T, right)


def run(kernel, shapes, *args, scratch=()):
    vmem = pl.BlockSpec(memory_space=pltpu.VMEM)
    several = isinstance(shapes[0], tuple)
    outs = [jax.ShapeDtypeStruct(s, jnp.float32) for s in (shapes if several else (shapes,))]
    return pl.pallas_call(
        kernel,
        out_shape=outs if several else outs[0],
        in_specs=[vmem] * len(args),
        out_specs=[vmem] * len(outs) if several else vmem,
        scratch_shapes=scratch,
    )(*args)


def step(activations, grad_output, weight, start_basis):
    n_d, n_t = lax.axis_size(DP), lax.axis_size(TENSOR)
    tokens, features = activations.shape
    rows, hidden = weight.shape
    rank = start_basis.shape[1]
    few = rank // n_t
    f32 = jnp.float32
    input_grad = input_gradient(grad_output, weight)
    mixed = run(mixed_kernel, (n_t, few, tokens), start_basis.T, grad_output)
    mixed = swap(mixed, TENSOR)
    left_part = run(left_kernel, (n_d, few, rows), mixed, activations, scratch=[pltpu.VMEM((16, tokens), f32)])
    left_mine = swap(left_part, DP)
    left_mine = left_mine.sum(axis=0)
    left_few = share(left_mine, DP)
    left_few = jnp.swapaxes(left_few, 0, 1).reshape(few, features)
    a32 = activations.astype(f32)
    seen = lax.dot_general(left_few, a32, (((1,), (1,)), ((), ())), precision=HIGH)
    both = share(jnp.concatenate([seen, left_mine], axis=1), TENSOR)
    both = both.reshape(rank, tokens + rows)
    width = hidden + 128
    packed = run(right_kernel, (n_d, rank // n_d, width), both, grad_output)
    packed = swap(packed, DP)
    packed = packed.sum(axis=0)
    packed = share(packed, DP)
    packed = packed.reshape(rank, width)
    right_basis, new_weight = run(
        functools.partial(last_kernel, tokens * n_d), ((rank, hidden), (rows, hidden)), packed, both[:, tokens:], weight
    )
    return (input_grad, right_basis.T, new_weight)


def solution(mesh):
    finer = Mesh(mesh.devices.reshape(4, 8, 8, 2), ("x", "z", "y", "c"))
    in_specs = (P(DP, None), P(DP, TENSOR), P(DP, TENSOR), P(TENSOR, None))
    out_specs = (P(DP, TENSOR), P(TENSOR, None), P(DP, TENSOR))
    return jax.shard_map(step, mesh=finer, in_specs=in_specs, out_specs=out_specs, check_vma=False)
```

```python
import functools

import jax
import jax.numpy as jnp
from jax import lax
from jax.experimental import pallas as pl
from jax.experimental.pallas import tpu as pltpu
from jax.sharding import Mesh
from jax.sharding import PartitionSpec as P


DP = ("x", "z")
TENSOR = ("y", "c")
HIGH = lax.Precision.HIGHEST

learn_rate = 0.001


def swap(parts, axis):
    return lax.all_to_all(parts, axis, split_axis=0, concat_axis=0, tiled=True)


def share(x, axis):
    return swap(jnp.broadcast_to(x[None], (lax.axis_size(axis), *x.shape)), axis)


def shifted(x, axis, by):
    length = lax.axis_size(axis)
    return lax.ppermute(x, axis, [(i, (i + by) % length) for i in range(length)])


def block_kernel(n_x, where, *refs):
    grads, weights = refs[:n_x], refs[n_x]
    earlier, parts = refs[n_x + 1 : -1], refs[-1]
    x, side = where[0], where[1]
    _, rows, hidden = weights.shape
    dims = (((1,), (1,)), ((), ()))
    for h in range(2):
        block = weights[pl.ds(4 * h + 2 * side, 2)].reshape(2 * rows, hidden)
        for s in range(n_x):
            total = lax.dot_general(grads[s][...], block, dims, preferred_element_type=jnp.float32)
            place = 2 * lax.rem(x - s + n_x, n_x) + h
            if earlier:
                total += earlier[0][place].astype(jnp.float32)
            parts[place] = total.astype(jnp.bfloat16)


def block_products(side, grads, weights, earlier=()):
    n_x, n_y = lax.axis_size("x"), lax.axis_size("y")
    tokens, rows = grads[0].shape[0], weights.shape[1]
    vmem = pl.BlockSpec(memory_space=pltpu.VMEM)
    where = jnp.stack([lax.axis_index("x"), side]).astype(jnp.int32)
    return pl.pallas_call(
        functools.partial(block_kernel, n_x),
        out_shape=jax.ShapeDtypeStruct((n_y, tokens, 2 * rows), jnp.bfloat16),
        in_specs=[pl.BlockSpec(memory_space=pltpu.SMEM)] + [vmem] * (n_x + 1 + len(earlier)),
        out_specs=vmem,
        name="blocks",
    )(where, *grads, weights, *earlier)


def input_gradient(grad_output, weight):
    n_x, n_y = lax.axis_size("x"), lax.axis_size("y")
    core = lax.axis_index("c")
    weights = lax.all_gather(weight, "z", axis=0)
    grads = [grad_output]
    for s in range(1, n_x):
        grads.append(shifted(grad_output, "x", s))
    give = block_products(1 - core, grads, weights)
    arrived = shifted(give, "c", 1)
    parts = block_products(core, grads, weights, (arrived,))
    summed = lax.psum_scatter(parts, "y", scatter_dimension=0)
    to = []
    for x in range(n_x):
        for y in range(n_y):
            for c in range(2):
                to.append(((x * n_y + y) * 2 + c, ((y // 2) * n_y + 2 * x + y % 2) * 2 + c))
    return lax.ppermute(summed, ("x", "y", "c"), to)


def thirds(value):
    first = value.astype(jnp.bfloat16)
    rest = value - first.astype(jnp.float32)
    second = rest.astype(jnp.bfloat16)
    third = (rest - second.astype(jnp.float32)).astype(jnp.bfloat16)
    return first, second, third


def exact_dot(value, other, dims):
    dot = functools.partial(lax.dot_general, dimension_numbers=(dims, ((), ())), preferred_element_type=jnp.float32)
    count = value.shape[0]
    parts = dot(jnp.concatenate(thirds(value), axis=0), other)
    return (parts[2 * count :] + parts[count : 2 * count]) + parts[:count]


def mixed_kernel(basis, grads, out):
    mixed = exact_dot(basis[...], grads[...], ((1,), (1,)))
    few = out.shape[1]
    for t in range(out.shape[0]):
        out[t] = mixed[t * few : (t + 1) * few]


def left_kernel(arrived, activations, out, lines):
    few = arrived.shape[1]
    mixed = arrived[0]
    for t in range(1, arrived.shape[0]):
        mixed += arrived[t]
    for i, part in enumerate(thirds(mixed)):
        lines[i * few : (i + 1) * few] = part.astype(jnp.float32)
    dot = jnp.dot(lines[: 3 * few].astype(jnp.bfloat16), activations[...], preferred_element_type=jnp.float32)
    total = (dot[2 * few :] + dot[few : 2 * few]) + dot[:few]
    rows = out.shape[2]
    for d in range(out.shape[0]):
        out[d] = total[:, d * rows : (d + 1) * rows]


def seen_kernel(arrived, activations, mine, out, lines):
    n_d, few, rows = arrived.shape
    tokens = activations.shape[0]
    for d in range(n_d):
        lines[:few, d * rows : (d + 1) * rows] = arrived[d]
    left = lines[:few]
    for i, part in enumerate(thirds(left)):
        lines[i * few : (i + 1) * few] = part.astype(jnp.float32)
    dims = (((1,), (1,)), ((), ()))
    dot = lax.dot_general(
        lines[: 3 * few].astype(jnp.bfloat16), activations[...], dims, preferred_element_type=jnp.float32
    )
    seen = (dot[2 * few :] + dot[few : 2 * few]) + dot[:few]
    for t in range(out.shape[0]):
        out[t, :, :tokens] = seen
        out[t, :, tokens:] = mine[...]


def right_kernel(both, grads, out, left_rows, lines):
    tokens, hidden = grads.shape
    n_t, few, _ = both.shape
    rank = n_t * few
    for t in range(n_t):
        lines[t * few : (t + 1) * few] = both[t]
    right = exact_dot(lines[:, :tokens], grads[...], ((1,), (0,)))
    rows = lines[:, tokens:]
    left_rows[...] = rows
    gram = lax.dot_general(rows, rows, (((1,), (1,)), ((), ())), precision=HIGH, preferred_element_type=jnp.float32)
    few = out.shape[1]
    for d in range(out.shape[0]):
        out[d, :, :hidden] = right[d * few : (d + 1) * few]
        out[d, :, hidden : hidden + rank] = gram[d * few : (d + 1) * few]
        out[d, :, hidden + rank :] = jnp.zeros((few, out.shape[2] - hidden - rank), jnp.float32)


def last_kernel(token_total, arrived, left_rows, weight, right_basis, new_weight, packed):
    few = arrived.shape[1]
    for d in range(arrived.shape[0]):
        packed[d * few : (d + 1) * few] = arrived[d]
    rank = packed.shape[0]
    hidden = weight.shape[1]
    row = lax.broadcasted_iota(jnp.int32, (8, 2 * rank), 0)
    lane = lax.broadcasted_iota(jnp.int32, (8, 2 * rank), 1)
    blocks = []
    for j in range(rank // 8):
        gram = packed[8 * j : 8 * j + 8, hidden : hidden + 2 * rank]
        blocks.append(jnp.where(lane < rank, gram, jnp.where(lane - rank == row + 8 * j, 1.0, 0.0)))
    for k in range(rank):
        b, i = divmod(k, 8)
        pivot = blocks[b][i : i + 1]
        scaled = pivot / pivot[:, k : k + 1]
        for j in range(b, rank // 8):
            factor = blocks[j][:, k : k + 1]
            if j == b:
                factor = jnp.where(row[:, :1] > i, factor, 0.0)
            blocks[j] = blocks[j] - factor * scaled
    inverse = []
    for j, block in enumerate(blocks):
        pivots = jnp.sum(jnp.where(lane == row + 8 * j, block, 0.0), axis=1, keepdims=True)
        inverse.append(block / jnp.sqrt(pivots))
    inverse = jnp.concatenate(inverse, axis=0)[:, rank:]
    dot = functools.partial(jnp.dot, precision=HIGH, preferred_element_type=jnp.float32)
    right = dot(inverse, packed[:, :hidden])
    basis = dot(inverse, left_rows[...])
    right_basis[...] = right / jnp.sqrt(jnp.float32(token_total))
    new_weight[...] = weight[...].astype(jnp.float32) - learn_rate * dot(basis.T, right)


def run(kernel, shapes, *args, scratch=()):
    vmem = pl.BlockSpec(memory_space=pltpu.VMEM)
    several = isinstance(shapes[0], tuple)
    outs = [jax.ShapeDtypeStruct(s, jnp.float32) for s in (shapes if several else (shapes,))]
    return pl.pallas_call(
        kernel,
        out_shape=outs if several else outs[0],
        in_specs=[vmem] * len(args),
        out_specs=[vmem] * len(outs) if several else vmem,
        scratch_shapes=scratch,
    )(*args)


def step(activations, grad_output, weight, start_basis):
    n_d, n_t = lax.axis_size(DP), lax.axis_size(TENSOR)
    tokens, features = activations.shape
    rows, hidden = weight.shape
    rank = start_basis.shape[1]
    few = rank // n_t
    f32 = jnp.float32
    input_grad = input_gradient(grad_output, weight)
    mixed = run(mixed_kernel, (n_t, few, tokens), start_basis.T, grad_output)
    mixed = swap(mixed, TENSOR)
    left_part = run(left_kernel, (n_d, few, rows), mixed, activations, scratch=[pltpu.VMEM((16, tokens), f32)])
    left_mine = swap(left_part, DP)
    left_mine = left_mine.sum(axis=0)
    left_few = share(left_mine, DP)
    both = run(
        seen_kernel,
        (n_t, few, tokens + rows),
        left_few,
        activations,
        left_mine,
        scratch=[pltpu.VMEM((16, features), f32)],
    )
    both = swap(both, TENSOR)
    width = hidden + 128
    packed, left_rows = run(
        right_kernel,
        ((n_d, rank // n_d, width), (rank, rows)),
        both,
        grad_output,
        scratch=[pltpu.VMEM((rank, tokens + rows), f32)],
    )
    packed = swap(packed, DP)
    packed = packed.sum(axis=0)
    packed = share(packed, DP)
    right_basis, new_weight = run(
        functools.partial(last_kernel, tokens * n_d),
        ((rank, hidden), (rows, hidden)),
        packed,
        left_rows,
        weight,
        scratch=[pltpu.VMEM((rank, width), f32)],
    )
    return (input_grad, right_basis.T, new_weight)


def solution(mesh):
    finer = Mesh(mesh.devices.reshape(4, 8, 8, 2), ("x", "z", "y", "c"))
    in_specs = (P(DP, None), P(DP, TENSOR), P(DP, TENSOR), P(TENSOR, None))
    out_specs = (P(DP, TENSOR), P(TENSOR, None), P(DP, TENSOR))
    return jax.shard_map(step, mesh=finer, in_specs=in_specs, out_specs=out_specs, check_vma=False)
```

```python
import functools

import jax
import jax.numpy as jnp
from jax import lax
from jax.experimental import pallas as pl
from jax.experimental.pallas import tpu as pltpu
from jax.sharding import Mesh
from jax.sharding import PartitionSpec as P


DP = ("x", "z")
TENSOR = ("y", "c")
HIGH = lax.Precision.HIGHEST

learn_rate = 0.001


def swap(parts, axis):
    return lax.all_to_all(parts, axis, split_axis=0, concat_axis=0, tiled=True)


def share(x, axis):
    return swap(jnp.broadcast_to(x[None], (lax.axis_size(axis), *x.shape)), axis)


def shifted(x, axis, by):
    length = lax.axis_size(axis)
    return lax.ppermute(x, axis, [(i, (i + by) % length) for i in range(length)])


def block_kernel(n_x, where, *refs):
    grads, weights = refs[:n_x], refs[n_x]
    earlier, parts = refs[n_x + 1 : -1], refs[-1]
    x, side = where[0], where[1]
    _, rows, hidden = weights.shape
    dims = (((1,), (1,)), ((), ()))
    for h in range(2):
        block = weights[pl.ds(4 * h + 2 * side, 2)].reshape(2 * rows, hidden)
        for s in range(n_x):
            total = lax.dot_general(grads[s][...], block, dims, preferred_element_type=jnp.float32)
            place = 2 * lax.rem(x - s + n_x, n_x) + h
            if earlier:
                total += earlier[0][place].astype(jnp.float32)
            parts[place] = total.astype(jnp.bfloat16)


def block_products(side, grads, weights, earlier=()):
    n_x, n_y = lax.axis_size("x"), lax.axis_size("y")
    tokens, rows = grads[0].shape[0], weights.shape[1]
    vmem = pl.BlockSpec(memory_space=pltpu.VMEM)
    where = jnp.stack([lax.axis_index("x"), side]).astype(jnp.int32)
    held = [pltpu.with_memory_space_constraint(a, pltpu.VMEM) for a in (*grads, *earlier)]
    return pl.pallas_call(
        functools.partial(block_kernel, n_x),
        out_shape=jax.ShapeDtypeStruct((n_y, tokens, 2 * rows), jnp.bfloat16),
        in_specs=[pl.BlockSpec(memory_space=pltpu.SMEM)] + [vmem] * (n_x + 1 + len(earlier)),
        out_specs=vmem,
        compiler_params=pltpu.CompilerParams(vmem_limit_bytes=16 << 20),
        name="blocks",
    )(where, *held[:n_x], weights, *held[n_x:])


def input_gradient(grad_output, weight):
    n_x, n_y = lax.axis_size("x"), lax.axis_size("y")
    core = lax.axis_index("c")
    weights = lax.all_gather(weight, "z", axis=0)
    grads = [grad_output]
    for s in range(1, n_x):
        grads.append(shifted(grad_output, "x", s))
    give = block_products(1 - core, grads, weights)
    arrived = shifted(give, "c", 1)
    parts = block_products(core, grads, weights, (arrived,))
    summed = lax.psum_scatter(parts, "y", scatter_dimension=0)
    to = []
    for x in range(n_x):
        for y in range(n_y):
            for c in range(2):
                to.append(((x * n_y + y) * 2 + c, ((y // 2) * n_y + 2 * x + y % 2) * 2 + c))
    return lax.ppermute(summed, ("x", "y", "c"), to)


def thirds(value):
    first = value.astype(jnp.bfloat16)
    rest = value - first.astype(jnp.float32)
    second = rest.astype(jnp.bfloat16)
    third = (rest - second.astype(jnp.float32)).astype(jnp.bfloat16)
    return first, second, third


def exact_dot(value, other, dims):
    dot = functools.partial(lax.dot_general, dimension_numbers=(dims, ((), ())), preferred_element_type=jnp.float32)
    count = value.shape[0]
    parts = dot(jnp.concatenate(thirds(value), axis=0), other)
    return (parts[2 * count :] + parts[count : 2 * count]) + parts[:count]


def mixed_kernel(basis, grads, out):
    mixed = exact_dot(basis[...], grads[...], ((1,), (1,)))
    few = out.shape[1]
    for t in range(out.shape[0]):
        out[t] = mixed[t * few : (t + 1) * few]


def left_kernel(arrived, activations, out, lines):
    few = arrived.shape[1]
    mixed = arrived[0]
    for t in range(1, arrived.shape[0]):
        mixed += arrived[t]
    for i, part in enumerate(thirds(mixed)):
        lines[i * few : (i + 1) * few] = part.astype(jnp.float32)
    dot = jnp.dot(lines[: 3 * few].astype(jnp.bfloat16), activations[...], preferred_element_type=jnp.float32)
    total = (dot[2 * few :] + dot[few : 2 * few]) + dot[:few]
    rows = out.shape[2]
    for d in range(out.shape[0]):
        out[d] = total[:, d * rows : (d + 1) * rows]


def seen_kernel(arrived, activations, mine, out, lines):
    n_d, few, rows = arrived.shape
    tokens = activations.shape[0]
    for d in range(n_d):
        lines[:few, d * rows : (d + 1) * rows] = arrived[d]
    left = lines[:few]
    for i, part in enumerate(thirds(left)):
        lines[i * few : (i + 1) * few] = part.astype(jnp.float32)
    dims = (((1,), (1,)), ((), ()))
    dot = lax.dot_general(
        lines[: 3 * few].astype(jnp.bfloat16), activations[...], dims, preferred_element_type=jnp.float32
    )
    seen = (dot[2 * few :] + dot[few : 2 * few]) + dot[:few]
    for t in range(out.shape[0]):
        out[t, :, :tokens] = seen
        out[t, :, tokens:] = mine[...]


def right_kernel(both, grads, out, left_rows, lines):
    tokens, hidden = grads.shape
    n_t, few, _ = both.shape
    rank = n_t * few
    for t in range(n_t):
        lines[t * few : (t + 1) * few] = both[t]
    right = exact_dot(lines[:, :tokens], grads[...], ((1,), (0,)))
    rows = lines[:, tokens:]
    left_rows[...] = rows
    gram = lax.dot_general(rows, rows, (((1,), (1,)), ((), ())), precision=HIGH, preferred_element_type=jnp.float32)
    few = out.shape[1]
    for d in range(out.shape[0]):
        out[d, :, :hidden] = right[d * few : (d + 1) * few]
        out[d, :, hidden : hidden + rank] = gram[d * few : (d + 1) * few]
        out[d, :, hidden + rank :] = jnp.zeros((few, out.shape[2] - hidden - rank), jnp.float32)


def last_kernel(token_total, arrived, left_rows, weight, right_basis, new_weight, packed):
    few = arrived.shape[1]
    for d in range(arrived.shape[0]):
        packed[d * few : (d + 1) * few] = arrived[d]
    rank = packed.shape[0]
    hidden = weight.shape[1]
    row = lax.broadcasted_iota(jnp.int32, (8, 2 * rank), 0)
    lane = lax.broadcasted_iota(jnp.int32, (8, 2 * rank), 1)
    blocks = []
    for j in range(rank // 8):
        gram = packed[8 * j : 8 * j + 8, hidden : hidden + 2 * rank]
        blocks.append(jnp.where(lane < rank, gram, jnp.where(lane - rank == row + 8 * j, 1.0, 0.0)))
    for k in range(rank):
        b, i = divmod(k, 8)
        pivot = blocks[b][i : i + 1]
        scaled = pivot / pivot[:, k : k + 1]
        for j in range(b, rank // 8):
            factor = blocks[j][:, k : k + 1]
            if j == b:
                factor = jnp.where(row[:, :1] > i, factor, 0.0)
            blocks[j] = blocks[j] - factor * scaled
    inverse = []
    for j, block in enumerate(blocks):
        pivots = jnp.sum(jnp.where(lane == row + 8 * j, block, 0.0), axis=1, keepdims=True)
        inverse.append(block / jnp.sqrt(pivots))
    inverse = jnp.concatenate(inverse, axis=0)[:, rank:]
    dot = functools.partial(jnp.dot, precision=HIGH, preferred_element_type=jnp.float32)
    right = dot(inverse, packed[:, :hidden])
    basis = dot(inverse, left_rows[...])
    right_basis[...] = right / jnp.sqrt(jnp.float32(token_total))
    new_weight[...] = weight[...].astype(jnp.float32) - learn_rate * dot(basis.T, right)


def run(kernel, shapes, *args, scratch=()):
    vmem = pl.BlockSpec(memory_space=pltpu.VMEM)
    args = [pltpu.with_memory_space_constraint(a, pltpu.VMEM) for a in args]
    several = isinstance(shapes[0], tuple)
    outs = [jax.ShapeDtypeStruct(s, jnp.float32) for s in (shapes if several else (shapes,))]
    return pl.pallas_call(
        kernel,
        out_shape=outs if several else outs[0],
        in_specs=[vmem] * len(args),
        out_specs=[vmem] * len(outs) if several else vmem,
        scratch_shapes=scratch,
        compiler_params=pltpu.CompilerParams(vmem_limit_bytes=12 << 20),
    )(*args)


def step(activations, grad_output, weight, start_basis):
    n_d, n_t = lax.axis_size(DP), lax.axis_size(TENSOR)
    tokens, features = activations.shape
    rows, hidden = weight.shape
    rank = start_basis.shape[1]
    few = rank // n_t
    f32 = jnp.float32
    input_grad = input_gradient(grad_output, weight)
    mixed = run(mixed_kernel, (n_t, few, tokens), start_basis.T, grad_output)
    mixed = swap(mixed, TENSOR)
    left_part = run(left_kernel, (n_d, few, rows), mixed, activations, scratch=[pltpu.VMEM((16, tokens), f32)])
    left_mine = swap(left_part, DP)
    left_mine = left_mine.sum(axis=0)
    left_few = share(left_mine, DP)
    both = run(
        seen_kernel,
        (n_t, few, tokens + rows),
        left_few,
        activations,
        left_mine,
        scratch=[pltpu.VMEM((16, features), f32)],
    )
    both = swap(both, TENSOR)
    width = hidden + 128
    packed, left_rows = run(
        right_kernel,
        ((n_d, rank // n_d, width), (rank, rows)),
        both,
        grad_output,
        scratch=[pltpu.VMEM((rank, tokens + rows), f32)],
    )
    packed = swap(packed, DP)
    packed = packed.sum(axis=0)
    packed = share(packed, DP)
    right_basis, new_weight = run(
        functools.partial(last_kernel, tokens * n_d),
        ((rank, hidden), (rows, hidden)),
        packed,
        left_rows,
        weight,
        scratch=[pltpu.VMEM((rank, width), f32)],
    )
    return (input_grad, right_basis.T, new_weight)


def solution(mesh):
    finer = Mesh(mesh.devices.reshape(4, 8, 8, 2), ("x", "z", "y", "c"))
    in_specs = (P(DP, None), P(DP, TENSOR), P(DP, TENSOR), P(TENSOR, None))
    out_specs = (P(DP, TENSOR), P(TENSOR, None), P(DP, TENSOR))
    return jax.shard_map(step, mesh=finer, in_specs=in_specs, out_specs=out_specs, check_vma=False)
```

```python
import functools

import jax
import jax.numpy as jnp
from jax import lax
from jax.experimental import pallas as pl
from jax.experimental.pallas import tpu as pltpu
from jax.sharding import Mesh
from jax.sharding import PartitionSpec as P


DP = ("x", "z")
TENSOR = ("y", "c")
HIGH = lax.Precision.HIGHEST

learn_rate = 0.001


def swap(parts, axis):
    return lax.all_to_all(parts, axis, split_axis=0, concat_axis=0, tiled=True)


def share(x, axis):
    return swap(jnp.broadcast_to(x[None], (lax.axis_size(axis), *x.shape)), axis)


def shifted(x, axis, by):
    length = lax.axis_size(axis)
    return lax.ppermute(x, axis, [(i, (i + by) % length) for i in range(length)])


def block_kernel(n_x, where, *refs):
    grads, weights = refs[:n_x], refs[n_x]
    x, core = where[0], where[1]
    _, rows, hidden = weights.shape
    dims = (((1,), (1,)), ((), ()))
    for side, parts in ((1 - core, refs[n_x + 1]), (core, refs[n_x + 2])):
        for h in range(2):
            block = weights[pl.ds(4 * h + 2 * side, 2)].reshape(2 * rows, hidden)
            for s in range(n_x):
                total = lax.dot_general(grads[s][...], block, dims, preferred_element_type=jnp.float32)
                parts[2 * lax.rem(x - s + n_x, n_x) + h] = total.astype(jnp.bfloat16)


def block_products(grads, weights):
    n_x, n_y = lax.axis_size("x"), lax.axis_size("y")
    tokens, rows = grads[0].shape[0], weights.shape[1]
    vmem = pl.BlockSpec(memory_space=pltpu.VMEM)
    where = jnp.stack([lax.axis_index("x"), lax.axis_index("c")]).astype(jnp.int32)
    held = [pltpu.with_memory_space_constraint(a, pltpu.VMEM) for a in grads]
    return pl.pallas_call(
        functools.partial(block_kernel, n_x),
        out_shape=[space((n_y, tokens, 2 * rows), jnp.bfloat16) for space in (pltpu.HBM, pltpu.HBM)],
        in_specs=[pl.BlockSpec(memory_space=pltpu.SMEM)] + [vmem] * (n_x + 1),
        out_specs=[vmem] * 2,
        compiler_params=pltpu.CompilerParams(vmem_limit_bytes=16 << 20),
        name="blocks",
    )(where, *held, weights)


def input_gradient(grad_output, weight):
    n_x, n_y = lax.axis_size("x"), lax.axis_size("y")
    weights = lax.all_gather(weight, "z", axis=0)
    grads = [grad_output]
    for s in range(1, n_x):
        grads.append(shifted(grad_output, "x", s))
    give, keep = block_products(grads, weights)
    arrived = shifted(give, "c", 1)
    parts = (keep.astype(jnp.float32) + arrived.astype(jnp.float32)).astype(jnp.bfloat16)
    summed = lax.psum_scatter(parts, "y", scatter_dimension=0)
    to = []
    for x in range(n_x):
        for y in range(n_y):
            for c in range(2):
                to.append(((x * n_y + y) * 2 + c, ((y // 2) * n_y + 2 * x + y % 2) * 2 + c))
    return lax.ppermute(summed, ("x", "y", "c"), to)


def thirds(value):
    first = value.astype(jnp.bfloat16)
    rest = value - first.astype(jnp.float32)
    second = rest.astype(jnp.bfloat16)
    third = (rest - second.astype(jnp.float32)).astype(jnp.bfloat16)
    return first, second, third


def exact_dot(value, other, dims):
    dot = functools.partial(lax.dot_general, dimension_numbers=(dims, ((), ())), preferred_element_type=jnp.float32)
    count = value.shape[0]
    parts = dot(jnp.concatenate(thirds(value), axis=0), other)
    return (parts[2 * count :] + parts[count : 2 * count]) + parts[:count]


def mixed_kernel(basis, grads, out):
    mixed = exact_dot(basis[...], grads[...], ((1,), (1,)))
    few = out.shape[1]
    for t in range(out.shape[0]):
        out[t] = mixed[t * few : (t + 1) * few]


def left_kernel(arrived, activations, out, lines):
    few = arrived.shape[1]
    mixed = arrived[0]
    for t in range(1, arrived.shape[0]):
        mixed += arrived[t]
    for i, part in enumerate(thirds(mixed)):
        lines[i * few : (i + 1) * few] = part.astype(jnp.float32)
    dot = jnp.dot(lines[: 3 * few].astype(jnp.bfloat16), activations[...], preferred_element_type=jnp.float32)
    total = (dot[2 * few :] + dot[few : 2 * few]) + dot[:few]
    rows = out.shape[2]
    for d in range(out.shape[0]):
        out[d] = total[:, d * rows : (d + 1) * rows]


def seen_kernel(arrived, activations, mine, out, lines):
    n_d, few, rows = arrived.shape
    tokens = activations.shape[0]
    for d in range(n_d):
        lines[:few, d * rows : (d + 1) * rows] = arrived[d]
    left = lines[:few]
    for i, part in enumerate(thirds(left)):
        lines[i * few : (i + 1) * few] = part.astype(jnp.float32)
    dims = (((1,), (1,)), ((), ()))
    dot = lax.dot_general(
        lines[: 3 * few].astype(jnp.bfloat16), activations[...], dims, preferred_element_type=jnp.float32
    )
    seen = (dot[2 * few :] + dot[few : 2 * few]) + dot[:few]
    for t in range(out.shape[0]):
        out[t, :, :tokens] = seen
        out[t, :, tokens:] = mine[...]


def right_kernel(both, grads, out, left_rows, lines):
    tokens, hidden = grads.shape
    n_t, few, _ = both.shape
    rank = n_t * few
    for t in range(n_t):
        lines[t * few : (t + 1) * few] = both[t]
    right = exact_dot(lines[:, :tokens], grads[...], ((1,), (0,)))
    rows = lines[:, tokens:]
    left_rows[...] = rows
    gram = lax.dot_general(rows, rows, (((1,), (1,)), ((), ())), precision=HIGH, preferred_element_type=jnp.float32)
    few = out.shape[1]
    for d in range(out.shape[0]):
        out[d, :, :hidden] = right[d * few : (d + 1) * few]
        out[d, :, hidden : hidden + rank] = gram[d * few : (d + 1) * few]
        out[d, :, hidden + rank :] = jnp.zeros((few, out.shape[2] - hidden - rank), jnp.float32)


def last_kernel(token_total, arrived, left_rows, weight, right_basis, new_weight, packed):
    few = arrived.shape[1]
    for d in range(arrived.shape[0]):
        packed[d * few : (d + 1) * few] = arrived[d]
    rank = packed.shape[0]
    hidden = weight.shape[1]
    row = lax.broadcasted_iota(jnp.int32, (8, 2 * rank), 0)
    lane = lax.broadcasted_iota(jnp.int32, (8, 2 * rank), 1)
    blocks = []
    for j in range(rank // 8):
        gram = packed[8 * j : 8 * j + 8, hidden : hidden + 2 * rank]
        blocks.append(jnp.where(lane < rank, gram, jnp.where(lane - rank == row + 8 * j, 1.0, 0.0)))
    for k in range(rank):
        b, i = divmod(k, 8)
        pivot = blocks[b][i : i + 1]
        scaled = pivot / pivot[:, k : k + 1]
        for j in range(b, rank // 8):
            factor = blocks[j][:, k : k + 1]
            if j == b:
                factor = jnp.where(row[:, :1] > i, factor, 0.0)
            blocks[j] = blocks[j] - factor * scaled
    inverse = []
    for j, block in enumerate(blocks):
        pivots = jnp.sum(jnp.where(lane == row + 8 * j, block, 0.0), axis=1, keepdims=True)
        inverse.append(block / jnp.sqrt(pivots))
    inverse = jnp.concatenate(inverse, axis=0)[:, rank:]
    dot = functools.partial(jnp.dot, precision=HIGH, preferred_element_type=jnp.float32)
    right = dot(inverse, packed[:, :hidden])
    basis = dot(inverse, left_rows[...])
    right_basis[...] = right / jnp.sqrt(jnp.float32(token_total))
    new_weight[...] = weight[...].astype(jnp.float32) - learn_rate * dot(basis.T, right)


def hold_kernel(source, out, done):
    copy = pltpu.make_async_copy(source, out, done)
    copy.start()
    copy.wait()


def hold(x):
    return pl.pallas_call(
        hold_kernel,
        out_shape=pltpu.VMEM(x.shape, x.dtype),
        in_specs=[pl.BlockSpec(memory_space=pl.ANY)],
        out_specs=pl.BlockSpec(memory_space=pltpu.VMEM),
        scratch_shapes=[pltpu.SemaphoreType.DMA],
        compiler_params=pltpu.CompilerParams(vmem_limit_bytes=4 << 20),
        name="hold",
    )(pltpu.with_memory_space_constraint(x, pltpu.HBM))


def run(kernel, shapes, *args, scratch=(), held=True):
    vmem = pl.BlockSpec(memory_space=pltpu.VMEM)
    space = pltpu.VMEM if held else pltpu.HBM
    args = [pltpu.with_memory_space_constraint(a, space) for a in args]
    several = isinstance(shapes[0], tuple)
    outs = [jax.ShapeDtypeStruct(s, jnp.float32) for s in (shapes if several else (shapes,))]
    return pl.pallas_call(
        kernel,
        out_shape=outs if several else outs[0],
        in_specs=[vmem] * len(args),
        out_specs=[vmem] * len(outs) if several else vmem,
        scratch_shapes=scratch,
        compiler_params=pltpu.CompilerParams(vmem_limit_bytes=12 << 20),
    )(*args)


def step(activations, grad_output, weight, start_basis):
    n_d, n_t = lax.axis_size(DP), lax.axis_size(TENSOR)
    tokens, features = activations.shape
    rows, hidden = weight.shape
    rank = start_basis.shape[1]
    few = rank // n_t
    f32 = jnp.float32
    input_grad = input_gradient(grad_output, weight)
    mixed = run(mixed_kernel, (n_t, few, tokens), start_basis.T, grad_output, held=False)
    activations = hold(activations)
    mixed = swap(mixed, TENSOR)
    left_part = run(left_kernel, (n_d, few, rows), mixed, activations, scratch=[pltpu.VMEM((16, tokens), f32)])
    left_mine = swap(left_part, DP)
    left_mine = left_mine.sum(axis=0)
    left_few = share(left_mine, DP)
    both = run(
        seen_kernel,
        (n_t, few, tokens + rows),
        left_few,
        activations,
        left_mine,
        scratch=[pltpu.VMEM((16, features), f32)],
    )
    both = swap(both, TENSOR)
    width = hidden + 128
    packed, left_rows = run(
        right_kernel,
        ((n_d, rank // n_d, width), (rank, rows)),
        both,
        grad_output,
        scratch=[pltpu.VMEM((rank, tokens + rows), f32)],
    )
    packed = swap(packed, DP)
    packed = packed.sum(axis=0)
    packed = share(packed, DP)
    right_basis, new_weight = run(
        functools.partial(last_kernel, tokens * n_d),
        ((rank, hidden), (rows, hidden)),
        packed,
        left_rows,
        weight,
        scratch=[pltpu.VMEM((rank, width), f32)],
    )
    return (input_grad, right_basis.T, new_weight)


def solution(mesh):
    finer = Mesh(mesh.devices.reshape(4, 8, 8, 2), ("x", "z", "y", "c"))
    in_specs = (P(DP, None), P(DP, TENSOR), P(DP, TENSOR), P(TENSOR, None))
    out_specs = (P(DP, TENSOR), P(TENSOR, None), P(DP, TENSOR))
    return jax.shard_map(step, mesh=finer, in_specs=in_specs, out_specs=out_specs, check_vma=False)
```

```python
import functools

import jax
import jax.numpy as jnp
from jax import lax
from jax.experimental import pallas as pl
from jax.experimental.pallas import tpu as pltpu
from jax.sharding import Mesh
from jax.sharding import PartitionSpec as P


DP = ("x", "z")
TENSOR = ("y", "c")
HIGH = lax.Precision.HIGHEST

learn_rate = 0.001


def swap(parts, axis):
    return lax.all_to_all(parts, axis, split_axis=0, concat_axis=0, tiled=True)


def shifted(x, axis, by):
    length = lax.axis_size(axis)
    return lax.ppermute(x, axis, [(i, (i + by) % length) for i in range(length)])


def block_kernel(n_x, where, *refs):
    grads, weights = refs[:n_x], refs[n_x]
    give, keep, held, sent, arrive, leave = refs[n_x + 1 :]
    x, core = where[0], where[1]
    _, rows, hidden = weights.shape
    dims = (((1,), (1,)), ((), ()))
    order = [(side, h) for side in range(2) for h in range(2)]
    coming, going = [], []
    for i, (side, h) in enumerate(order):
        first = 4 * h + 2 * (core if side else 1 - core)
        copy = pltpu.make_async_copy(weights.at[pl.ds(first, 2)], held.at[i], arrive.at[i])
        copy.start()
        coming.append(copy)
    for i, (side, h) in enumerate(order):
        coming[i].wait()
        block = held[i].reshape(2 * rows, hidden)
        for s in range(n_x):
            total = lax.dot_general(grads[s][...], block, dims, preferred_element_type=jnp.float32)
            place = 2 * lax.rem(x - s + n_x, n_x) + h
            k = i * n_x + s
            sent[k] = total.astype(jnp.bfloat16)
            copy = pltpu.make_async_copy(sent.at[k], (keep if side else give).at[place], leave.at[k])
            copy.start()
            going.append(copy)
    for copy in going:
        copy.wait()


def add_kernel(mine, other, out):
    out[...] = (mine[...].astype(jnp.float32) + other[...].astype(jnp.float32)).astype(jnp.bfloat16)


def added(mine, other):
    args = [pltpu.with_memory_space_constraint(a, pltpu.HBM) for a in (mine, other)]
    block = pl.BlockSpec((2, *mine.shape[1:]), lambda i: (i, 0, 0))
    return pl.pallas_call(
        add_kernel,
        grid=(mine.shape[0] // 2,),
        out_shape=pltpu.HBM(mine.shape, mine.dtype),
        in_specs=[block] * 2,
        out_specs=block,
        compiler_params=pltpu.CompilerParams(vmem_limit_bytes=8 << 20),
        name="added",
    )(*args)


def block_products(grads, weights):
    n_x, n_y = lax.axis_size("x"), lax.axis_size("y")
    tokens = grads[0].shape[0]
    _, rows, hidden = weights.shape
    vmem = pl.BlockSpec(memory_space=pltpu.VMEM)
    anywhere = pl.BlockSpec(memory_space=pl.ANY)
    where = jnp.stack([lax.axis_index("x"), lax.axis_index("c")]).astype(jnp.int32)
    held = [pltpu.with_memory_space_constraint(a, pltpu.VMEM) for a in grads]
    parts = (n_y, tokens, 2 * rows)
    return pl.pallas_call(
        functools.partial(block_kernel, n_x),
        out_shape=[pltpu.HBM(parts, jnp.bfloat16)] * 2,
        in_specs=[pl.BlockSpec(memory_space=pltpu.SMEM)] + [vmem] * n_x + [anywhere],
        out_specs=[anywhere] * 2,
        scratch_shapes=[
            pltpu.VMEM((4, 2, rows, hidden), jnp.bfloat16),
            pltpu.VMEM((2 * n_y, *parts[1:]), jnp.bfloat16),
            pltpu.SemaphoreType.DMA((4,)),
            pltpu.SemaphoreType.DMA((2 * n_y,)),
        ],
        compiler_params=pltpu.CompilerParams(vmem_limit_bytes=12 << 20),
        name="blocks",
    )(where, *held, pltpu.with_memory_space_constraint(weights, pltpu.HBM))


def input_gradient(grad_output, weight):
    n_x, n_y = lax.axis_size("x"), lax.axis_size("y")
    weights = lax.all_gather(weight, "z", axis=0)
    grads = [grad_output]
    for s in range(1, n_x):
        grads.append(shifted(grad_output, "x", s))
    give, keep = block_products(grads, weights)
    arrived = shifted(give, "c", 1)
    parts = added(keep, arrived)
    summed = lax.psum_scatter(parts, "y", scatter_dimension=0)
    to = []
    for x in range(n_x):
        for y in range(n_y):
            for c in range(2):
                to.append(((x * n_y + y) * 2 + c, ((y // 2) * n_y + 2 * x + y % 2) * 2 + c))
    return lax.ppermute(summed, ("x", "y", "c"), to)


def thirds(value):
    first = value.astype(jnp.bfloat16)
    rest = value - first.astype(jnp.float32)
    second = rest.astype(jnp.bfloat16)
    third = (rest - second.astype(jnp.float32)).astype(jnp.bfloat16)
    return first, second, third


def exact_dot(value, other, dims):
    dot = functools.partial(lax.dot_general, dimension_numbers=(dims, ((), ())), preferred_element_type=jnp.float32)
    count = value.shape[0]
    parts = dot(jnp.concatenate(thirds(value), axis=0), other)
    return (parts[2 * count :] + parts[count : 2 * count]) + parts[:count]


def mixed_kernel(basis, grads, out):
    mixed = exact_dot(basis[...], grads[...], ((1,), (1,)))
    few = out.shape[1]
    for t in range(out.shape[0]):
        out[t] = mixed[t * few : (t + 1) * few]


def left_kernel(arrived, activations, out, lines):
    few = arrived.shape[1]
    mixed = arrived[0]
    for t in range(1, arrived.shape[0]):
        mixed += arrived[t]
    for i, part in enumerate(thirds(mixed)):
        lines[i * few : (i + 1) * few] = part.astype(jnp.float32)
    dot = jnp.dot(lines[: 3 * few].astype(jnp.bfloat16), activations[...], preferred_element_type=jnp.float32)
    total = (dot[2 * few :] + dot[few : 2 * few]) + dot[:few]
    rows = out.shape[2]
    for d in range(out.shape[0]):
        out[d] = total[:, d * rows : (d + 1) * rows]


def seen_kernel(arrived, activations, mine, out, lines):
    n_d, few, rows = arrived.shape
    tokens = activations.shape[0]
    for d in range(n_d):
        lines[:few, d * rows : (d + 1) * rows] = arrived[d]
    left = lines[:few]
    for i, part in enumerate(thirds(left)):
        lines[i * few : (i + 1) * few] = part.astype(jnp.float32)
    dims = (((1,), (1,)), ((), ()))
    dot = lax.dot_general(
        lines[: 3 * few].astype(jnp.bfloat16), activations[...], dims, preferred_element_type=jnp.float32
    )
    seen = (dot[2 * few :] + dot[few : 2 * few]) + dot[:few]
    for t in range(out.shape[0]):
        out[t, :, :tokens] = seen
        out[t, :, tokens:] = mine[...]


def right_kernel(both, grads, out, left_rows, lines):
    tokens, hidden = grads.shape
    n_t, few, _ = both.shape
    rank = n_t * few
    for t in range(n_t):
        lines[t * few : (t + 1) * few] = both[t]
    right = exact_dot(lines[:, :tokens], grads[...], ((1,), (0,)))
    rows = lines[:, tokens:]
    left_rows[...] = rows
    gram = lax.dot_general(rows, rows, (((1,), (1,)), ((), ())), precision=HIGH, preferred_element_type=jnp.float32)
    few = out.shape[1]
    for d in range(out.shape[0]):
        out[d, :, :hidden] = right[d * few : (d + 1) * few]
        out[d, :, hidden : hidden + rank] = gram[d * few : (d + 1) * few]
        out[d, :, hidden + rank :] = jnp.zeros((few, out.shape[2] - hidden - rank), jnp.float32)


def spread_kernel(arrived, mine, out):
    total = arrived[0]
    for d in range(1, arrived.shape[0]):
        total += arrived[d]
    mine[...] = total
    for d in range(out.shape[0]):
        out[d] = total


def last_kernel(token_total, arrived, left_rows, weight, right_basis, new_weight, packed):
    few = arrived.shape[1]
    for d in range(arrived.shape[0]):
        packed[d * few : (d + 1) * few] = arrived[d]
    rank = packed.shape[0]
    hidden = weight.shape[1]
    row = lax.broadcasted_iota(jnp.int32, (8, 2 * rank), 0)
    lane = lax.broadcasted_iota(jnp.int32, (8, 2 * rank), 1)
    blocks = []
    for j in range(rank // 8):
        gram = packed[8 * j : 8 * j + 8, hidden : hidden + 2 * rank]
        blocks.append(jnp.where(lane < rank, gram, jnp.where(lane - rank == row + 8 * j, 1.0, 0.0)))
    for k in range(rank):
        b, i = divmod(k, 8)
        pivot = blocks[b][i : i + 1]
        scaled = pivot / pivot[:, k : k + 1]
        for j in range(b, rank // 8):
            factor = blocks[j][:, k : k + 1]
            if j == b:
                factor = jnp.where(row[:, :1] > i, factor, 0.0)
            blocks[j] = blocks[j] - factor * scaled
    inverse = []
    for j, block in enumerate(blocks):
        pivots = jnp.sum(jnp.where(lane == row + 8 * j, block, 0.0), axis=1, keepdims=True)
        inverse.append(block / jnp.sqrt(pivots))
    inverse = jnp.concatenate(inverse, axis=0)[:, rank:]
    dot = functools.partial(jnp.dot, precision=HIGH, preferred_element_type=jnp.float32)
    right = dot(inverse, packed[:, :hidden])
    basis = dot(inverse, left_rows[...])
    right_basis[...] = right / jnp.sqrt(jnp.float32(token_total))
    new_weight[...] = weight[...].astype(jnp.float32) - learn_rate * dot(basis.T, right)


def hold_kernel(source, out, done):
    copy = pltpu.make_async_copy(source, out, done)
    copy.start()
    copy.wait()


def hold(x):
    return pl.pallas_call(
        hold_kernel,
        out_shape=pltpu.VMEM(x.shape, x.dtype),
        in_specs=[pl.BlockSpec(memory_space=pl.ANY)],
        out_specs=pl.BlockSpec(memory_space=pltpu.VMEM),
        scratch_shapes=[pltpu.SemaphoreType.DMA],
        compiler_params=pltpu.CompilerParams(vmem_limit_bytes=4 << 20),
        name="hold",
    )(pltpu.with_memory_space_constraint(x, pltpu.HBM))


def run(kernel, shapes, *args, scratch=(), held=True, out=jax.ShapeDtypeStruct):
    vmem = pl.BlockSpec(memory_space=pltpu.VMEM)
    space = pltpu.VMEM if held else pltpu.HBM
    args = [pltpu.with_memory_space_constraint(a, space) for a in args]
    several = isinstance(shapes[0], tuple)
    outs = [out(s, jnp.float32) for s in (shapes if several else (shapes,))]
    return pl.pallas_call(
        kernel,
        out_shape=outs if several else outs[0],
        in_specs=[vmem] * len(args),
        out_specs=[vmem] * len(outs) if several else vmem,
        scratch_shapes=scratch,
        compiler_params=pltpu.CompilerParams(vmem_limit_bytes=12 << 20),
    )(*args)


def step(activations, grad_output, weight, start_basis):
    n_d, n_t = lax.axis_size(DP), lax.axis_size(TENSOR)
    tokens, features = activations.shape
    rows, hidden = weight.shape
    rank = start_basis.shape[1]
    few = rank // n_t
    f32 = jnp.float32
    input_grad = input_gradient(grad_output, weight)
    mixed = run(mixed_kernel, (n_t, few, tokens), start_basis.T, grad_output, held=False)
    activations = hold(activations)
    mixed = swap(mixed, TENSOR)
    left_part = run(left_kernel, (n_d, few, rows), mixed, activations, scratch=[pltpu.VMEM((16, tokens), f32)])
    left_mine = swap(left_part, DP)
    left_mine, left_few = run(spread_kernel, ((few, rows), (n_d, few, rows)), left_mine, out=pltpu.HBM)
    left_few = swap(left_few, DP)
    both = run(
        seen_kernel,
        (n_t, few, tokens + rows),
        left_few,
        activations,
        left_mine,
        scratch=[pltpu.VMEM((16, features), f32)],
    )
    both = swap(both, TENSOR)
    width = hidden + 128
    packed, left_rows = run(
        right_kernel,
        ((n_d, rank // n_d, width), (rank, rows)),
        both,
        grad_output,
        scratch=[pltpu.VMEM((rank, tokens + rows), f32)],
    )
    packed = swap(packed, DP)
    _, packed = run(spread_kernel, ((rank // n_d, width), (n_d, rank // n_d, width)), packed, out=pltpu.HBM)
    packed = swap(packed, DP)
    right_basis, new_weight = run(
        functools.partial(last_kernel, tokens * n_d),
        ((rank, hidden), (rows, hidden)),
        packed,
        left_rows,
        weight,
        scratch=[pltpu.VMEM((rank, width), f32)],
    )
    return (input_grad, right_basis.T, new_weight)


def solution(mesh):
    finer = Mesh(mesh.devices.reshape(4, 8, 8, 2), ("x", "z", "y", "c"))
    in_specs = (P(DP, None), P(DP, TENSOR), P(DP, TENSOR), P(TENSOR, None))
    out_specs = (P(DP, TENSOR), P(TENSOR, None), P(DP, TENSOR))
    return jax.shard_map(step, mesh=finer, in_specs=in_specs, out_specs=out_specs, check_vma=False)
```

```python
import functools

import jax
import jax.numpy as jnp
from jax import lax
from jax.experimental import pallas as pl
from jax.experimental.pallas import tpu as pltpu
from jax.sharding import Mesh
from jax.sharding import PartitionSpec as P


DP = ("x", "z")
TENSOR = ("y", "c")
HIGH = lax.Precision.HIGHEST

learn_rate = 0.001


def swap(parts, axis):
    return lax.all_to_all(parts, axis, split_axis=0, concat_axis=0, tiled=True)


def shifted(x, axis, by):
    length = lax.axis_size(axis)
    return lax.ppermute(x, axis, [(i, (i + by) % length) for i in range(length)])


def block_kernel(n_x, where, *refs):
    grads, weights = refs[:n_x], refs[n_x]
    give, keep, lines, held, sent, enter, arrive, leave = refs[n_x + 1 :]
    x, core = where[0], where[1]
    _, rows, hidden = weights.shape
    tokens = grads[0].shape[0]
    dims = (((1,), (1,)), ((), ()))
    order = [(side, h) for side in range(2) for h in range(2)]

    def bring_weights(i):
        side, h = order[i]
        first = 4 * h + 2 * (core if side else 1 - core)
        copy = pltpu.make_async_copy(weights.at[pl.ds(first, 2)], held.at[i], arrive.at[i])
        copy.start()
        return copy

    def bring_grads(s):
        copy = pltpu.make_async_copy(grads[s], lines.at[pl.ds(s * tokens, tokens)], enter.at[s])
        copy.start()
        return copy

    first = bring_weights(0)
    entering = [bring_grads(s) for s in range(n_x)]
    coming = [first] + [bring_weights(i) for i in range(1, len(order))]
    going = []
    for i, (side, h) in enumerate(order):
        coming[i].wait()
        block = held[i].reshape(2 * rows, hidden)
        step = 2 if i == 0 else n_x
        for start in range(0, n_x, step):
            if i == 0:
                for s in range(start, start + step):
                    entering[s].wait()
            total = lax.dot_general(
                lines[start * tokens : (start + step) * tokens], block, dims, preferred_element_type=jnp.float32
            )
            for s in range(start, start + step):
                k = i * n_x + s
                sent[k] = total[(s - start) * tokens : (s - start + 1) * tokens].astype(jnp.bfloat16)
                place = 2 * lax.rem(x - s + n_x, n_x) + h
                copy = pltpu.make_async_copy(sent.at[k], (keep if side else give).at[place], leave.at[k])
                copy.start()
                going.append(copy)
    for copy in going:
        copy.wait()


def block_products(grads, weights):
    n_x, n_y = lax.axis_size("x"), lax.axis_size("y")
    tokens = grads[0].shape[0]
    _, rows, hidden = weights.shape
    anywhere = pl.BlockSpec(memory_space=pl.ANY)
    where = jnp.stack([lax.axis_index("x"), lax.axis_index("c")]).astype(jnp.int32)
    args = [pltpu.with_memory_space_constraint(a, pltpu.HBM) for a in (*grads, weights)]
    parts = (n_y, tokens, 2 * rows)
    return pl.pallas_call(
        functools.partial(block_kernel, n_x),
        out_shape=[pltpu.HBM(parts, jnp.bfloat16)] * 2,
        in_specs=[pl.BlockSpec(memory_space=pltpu.SMEM)] + [anywhere] * (n_x + 1),
        out_specs=[anywhere] * 2,
        scratch_shapes=[
            pltpu.VMEM((n_x * tokens, hidden), jnp.bfloat16),
            pltpu.VMEM((4, 2, rows, hidden), jnp.bfloat16),
            pltpu.VMEM((2 * n_y, *parts[1:]), jnp.bfloat16),
            pltpu.SemaphoreType.DMA((n_x,)),
            pltpu.SemaphoreType.DMA((4,)),
            pltpu.SemaphoreType.DMA((2 * n_y,)),
        ],
        compiler_params=pltpu.CompilerParams(vmem_limit_bytes=20 << 20),
        name="blocks",
    )(where, *args)


def input_gradient(grad_output, weight):
    n_x, n_y = lax.axis_size("x"), lax.axis_size("y")
    weights = lax.all_gather(weight, "z", axis=0)
    grads = [grad_output]
    for s in range(1, n_x):
        grads.append(shifted(grad_output, "x", s))
    give, keep = block_products(grads, weights)
    arrived = shifted(give, "c", 1)
    parts = (keep.astype(jnp.float32) + arrived.astype(jnp.float32)).astype(jnp.bfloat16)
    summed = lax.psum_scatter(parts, "y", scatter_dimension=0)
    to = []
    for x in range(n_x):
        for y in range(n_y):
            for c in range(2):
                to.append(((x * n_y + y) * 2 + c, ((y // 2) * n_y + 2 * x + y % 2) * 2 + c))
    return lax.ppermute(summed, ("x", "y", "c"), to)


def thirds(value):
    first = value.astype(jnp.bfloat16)
    rest = value - first.astype(jnp.float32)
    second = rest.astype(jnp.bfloat16)
    third = (rest - second.astype(jnp.float32)).astype(jnp.bfloat16)
    return first, second, third


def exact_dot(value, other, dims):
    dot = functools.partial(lax.dot_general, dimension_numbers=(dims, ((), ())), preferred_element_type=jnp.float32)
    count = value.shape[0]
    parts = dot(jnp.concatenate(thirds(value), axis=0), other)
    return (parts[2 * count :] + parts[count : 2 * count]) + parts[:count]


def mixed_kernel(basis, grads, activations, out, held, done):
    copy = pltpu.make_async_copy(activations, held, done)
    copy.start()
    mixed = exact_dot(basis[...], grads[...], ((1,), (1,)))
    few = out.shape[1]
    for t in range(out.shape[0]):
        out[t] = mixed[t * few : (t + 1) * few]
    copy.wait()


def left_kernel(arrived, activations, out, lines):
    few = arrived.shape[1]
    mixed = arrived[0]
    for t in range(1, arrived.shape[0]):
        mixed += arrived[t]
    for i, part in enumerate(thirds(mixed)):
        lines[i * few : (i + 1) * few] = part.astype(jnp.float32)
    dot = jnp.dot(lines[: 3 * few].astype(jnp.bfloat16), activations[...], preferred_element_type=jnp.float32)
    total = (dot[2 * few :] + dot[few : 2 * few]) + dot[:few]
    rows = out.shape[2]
    for d in range(out.shape[0]):
        out[d] = total[:, d * rows : (d + 1) * rows]


def seen_kernel(arrived, activations, mine, out, lines):
    n_d, few, rows = arrived.shape
    tokens = activations.shape[0]
    for d in range(n_d):
        lines[:few, d * rows : (d + 1) * rows] = arrived[d]
    left = lines[:few]
    for i, part in enumerate(thirds(left)):
        lines[i * few : (i + 1) * few] = part.astype(jnp.float32)
    dims = (((1,), (1,)), ((), ()))
    dot = lax.dot_general(
        lines[: 3 * few].astype(jnp.bfloat16), activations[...], dims, preferred_element_type=jnp.float32
    )
    seen = (dot[2 * few :] + dot[few : 2 * few]) + dot[:few]
    for t in range(out.shape[0]):
        out[t, :, :tokens] = seen
        out[t, :, tokens:] = mine[...]


def right_kernel(both, grads, out, left_rows, lines):
    tokens, hidden = grads.shape
    n_t, few, _ = both.shape
    rank = n_t * few
    for t in range(n_t):
        lines[t * few : (t + 1) * few] = both[t]
    right = exact_dot(lines[:, :tokens], grads[...], ((1,), (0,)))
    rows = lines[:, tokens:]
    left_rows[...] = rows
    gram = lax.dot_general(rows, rows, (((1,), (1,)), ((), ())), precision=HIGH, preferred_element_type=jnp.float32)
    few = out.shape[1]
    for d in range(out.shape[0]):
        out[d, :, :hidden] = right[d * few : (d + 1) * few]
        out[d, :, hidden : hidden + rank] = gram[d * few : (d + 1) * few]
        out[d, :, hidden + rank :] = jnp.zeros((few, out.shape[2] - hidden - rank), jnp.float32)


def spread_kernel(arrived, mine, out):
    total = arrived[0]
    for d in range(1, arrived.shape[0]):
        total += arrived[d]
    mine[...] = total
    for d in range(out.shape[0]):
        out[d] = total


def factor_kernel(hidden, arrived, packed, out):
    few = arrived.shape[1]
    for d in range(arrived.shape[0]):
        packed[d * few : (d + 1) * few] = arrived[d]
    rank = packed.shape[0]
    row = lax.broadcasted_iota(jnp.int32, (8, 2 * rank), 0)
    lane = lax.broadcasted_iota(jnp.int32, (8, 2 * rank), 1)
    blocks = []
    for j in range(rank // 8):
        gram = packed[8 * j : 8 * j + 8, hidden : hidden + 2 * rank]
        blocks.append(jnp.where(lane < rank, gram, jnp.where(lane - rank == row + 8 * j, 1.0, 0.0)))
    for k in range(rank):
        b, i = divmod(k, 8)
        pivot = blocks[b][i : i + 1]
        scaled = pivot / pivot[:, k : k + 1]
        for j in range(b, rank // 8):
            factor = blocks[j][:, k : k + 1]
            if j == b:
                factor = jnp.where(row[:, :1] > i, factor, 0.0)
            blocks[j] = blocks[j] - factor * scaled
    inverse = []
    for j, block in enumerate(blocks):
        pivots = jnp.sum(jnp.where(lane == row + 8 * j, block, 0.0), axis=1, keepdims=True)
        inverse.append(block / jnp.sqrt(pivots))
    out[...] = jnp.concatenate(inverse, axis=0)


def last_kernel(token_total, packed, inverse, left_rows, weight, right_basis, new_weight):
    rank = packed.shape[0]
    hidden = weight.shape[1]
    inverse = inverse[:, rank:]
    dot = functools.partial(jnp.dot, precision=HIGH, preferred_element_type=jnp.float32)
    right = dot(inverse, packed[:, :hidden])
    basis = dot(inverse, left_rows[...])
    right_basis[...] = right / jnp.sqrt(jnp.float32(token_total))
    new_weight[...] = weight[...].astype(jnp.float32) - learn_rate * dot(basis.T, right)


def mixed_and_held(basis, grads, activations, shape):
    vmem = pl.BlockSpec(memory_space=pltpu.VMEM)
    args = [pltpu.with_memory_space_constraint(a, pltpu.HBM) for a in (basis, grads, activations)]
    return pl.pallas_call(
        mixed_kernel,
        out_shape=[pltpu.HBM(shape, jnp.float32), pltpu.VMEM(activations.shape, activations.dtype)],
        in_specs=[vmem] * 2 + [pl.BlockSpec(memory_space=pl.ANY)],
        out_specs=[vmem] * 2,
        scratch_shapes=[pltpu.SemaphoreType.DMA],
        compiler_params=pltpu.CompilerParams(vmem_limit_bytes=12 << 20),
        name="mixed",
    )(*args)


def run(kernel, shapes, *args, scratch=(), held=True, out=jax.ShapeDtypeStruct):
    vmem = pl.BlockSpec(memory_space=pltpu.VMEM)
    space = pltpu.VMEM if held else pltpu.HBM
    args = [pltpu.with_memory_space_constraint(a, space) for a in args]
    several = isinstance(shapes[0], tuple)
    outs = [out(s, jnp.float32) for s in (shapes if several else (shapes,))]
    return pl.pallas_call(
        kernel,
        out_shape=outs if several else outs[0],
        in_specs=[vmem] * len(args),
        out_specs=[vmem] * len(outs) if several else vmem,
        scratch_shapes=scratch,
        compiler_params=pltpu.CompilerParams(vmem_limit_bytes=12 << 20),
    )(*args)


def step(activations, grad_output, weight, start_basis):
    n_d, n_t = lax.axis_size(DP), lax.axis_size(TENSOR)
    tokens, features = activations.shape
    rows, hidden = weight.shape
    rank = start_basis.shape[1]
    few = rank // n_t
    f32 = jnp.float32
    input_grad = input_gradient(grad_output, weight)
    mixed, activations = mixed_and_held(start_basis.T, grad_output, activations, (n_t, few, tokens))
    mixed = swap(mixed, TENSOR)
    left_part = run(left_kernel, (n_d, few, rows), mixed, activations, scratch=[pltpu.VMEM((16, tokens), f32)])
    left_mine = swap(left_part, DP)
    left_mine, left_few = run(spread_kernel, ((few, rows), (n_d, few, rows)), left_mine, out=pltpu.HBM)
    left_few = swap(left_few, DP)
    both = run(
        seen_kernel,
        (n_t, few, tokens + rows),
        left_few,
        activations,
        left_mine,
        scratch=[pltpu.VMEM((16, features), f32)],
    )
    both = swap(both, TENSOR)
    width = hidden + 128
    packed, left_rows = run(
        right_kernel,
        ((n_d, rank // n_d, width), (rank, rows)),
        both,
        grad_output,
        scratch=[pltpu.VMEM((rank, tokens + rows), f32)],
    )
    packed = swap(packed, DP)
    _, packed = run(spread_kernel, ((rank // n_d, width), (n_d, rank // n_d, width)), packed, out=pltpu.HBM)
    packed = swap(packed, DP)
    packed, inverse = run(
        functools.partial(factor_kernel, hidden), ((rank, width), (rank, 2 * rank)), packed, out=pltpu.VMEM
    )
    right_basis, new_weight = run(
        functools.partial(last_kernel, tokens * n_d),
        ((rank, hidden), (rows, hidden)),
        packed,
        inverse,
        left_rows,
        weight,
    )
    return (input_grad, right_basis.T, new_weight)


def solution(mesh):
    finer = Mesh(mesh.devices.reshape(4, 8, 8, 2), ("x", "z", "y", "c"))
    in_specs = (P(DP, None), P(DP, TENSOR), P(DP, TENSOR), P(TENSOR, None))
    out_specs = (P(DP, TENSOR), P(TENSOR, None), P(DP, TENSOR))
    return jax.shard_map(step, mesh=finer, in_specs=in_specs, out_specs=out_specs, check_vma=False)
```

```python
import functools

import jax
import jax.numpy as jnp
from jax import lax
from jax.experimental import pallas as pl
from jax.experimental.pallas import tpu as pltpu
from jax.sharding import Mesh
from jax.sharding import PartitionSpec as P


DP = ("x", "z")
TENSOR = ("y", "c")
HIGH = lax.Precision.HIGHEST

learn_rate = 0.001


def swap(parts, axis):
    return lax.all_to_all(parts, axis, split_axis=0, concat_axis=0, tiled=True)


def shifted(x, axis, by):
    length = lax.axis_size(axis)
    return lax.ppermute(x, axis, [(i, (i + by) % length) for i in range(length)])


def block_kernel(n_x, where, *refs):
    grads, weights = refs[:n_x], refs[n_x]
    out, held, sent, arrive, leave = refs[n_x + 1 :]
    x, side = where[0], where[1]
    _, rows, hidden = weights.shape
    dims = (((1,), (1,)), ((), ()))
    coming, going = [], []
    for h in range(2):
        copy = pltpu.make_async_copy(weights.at[pl.ds(4 * h + 2 * side, 2)], held.at[h], arrive.at[h])
        copy.start()
        coming.append(copy)
    for h in range(2):
        coming[h].wait()
        block = held[h].reshape(2 * rows, hidden)
        for s in range(n_x):
            total = lax.dot_general(grads[s][...], block, dims, preferred_element_type=jnp.float32)
            k = h * n_x + s
            sent[k] = total.astype(jnp.bfloat16)
            place = 2 * lax.rem(x - s + n_x, n_x) + h
            copy = pltpu.make_async_copy(sent.at[k], out.at[place], leave.at[k])
            copy.start()
            going.append(copy)
    for copy in going:
        copy.wait()


def block_products(side, grads, weights):
    n_x, n_y = lax.axis_size("x"), lax.axis_size("y")
    tokens = grads[0].shape[0]
    _, rows, hidden = weights.shape
    vmem = pl.BlockSpec(memory_space=pltpu.VMEM)
    anywhere = pl.BlockSpec(memory_space=pl.ANY)
    where = jnp.stack([lax.axis_index("x"), side]).astype(jnp.int32)
    held = [pltpu.with_memory_space_constraint(a, pltpu.VMEM) for a in grads]
    parts = (n_y, tokens, 2 * rows)
    return pl.pallas_call(
        functools.partial(block_kernel, n_x),
        out_shape=pltpu.HBM(parts, jnp.bfloat16),
        in_specs=[pl.BlockSpec(memory_space=pltpu.SMEM)] + [vmem] * n_x + [anywhere],
        out_specs=anywhere,
        scratch_shapes=[
            pltpu.VMEM((2, 2, rows, hidden), jnp.bfloat16),
            pltpu.VMEM(parts, jnp.bfloat16),
            pltpu.SemaphoreType.DMA((2,)),
            pltpu.SemaphoreType.DMA((n_y,)),
        ],
        compiler_params=pltpu.CompilerParams(vmem_limit_bytes=8 << 20),
        name="blocks",
    )(where, *held, pltpu.with_memory_space_constraint(weights, pltpu.HBM))


def input_gradient(grad_output, weight):
    n_x, n_y = lax.axis_size("x"), lax.axis_size("y")
    weights = lax.all_gather(weight, "z", axis=0)
    grads = [grad_output]
    for s in range(1, n_x):
        grads.append(shifted(grad_output, "x", s))
    core = lax.axis_index("c")
    give = block_products(1 - core, grads, weights)
    arrived = shifted(give, "c", 1)
    keep = block_products(core, grads, weights)
    parts = (keep.astype(jnp.float32) + arrived.astype(jnp.float32)).astype(jnp.bfloat16)
    summed = lax.psum_scatter(parts, "y", scatter_dimension=0)
    to = []
    for x in range(n_x):
        for y in range(n_y):
            for c in range(2):
                to.append(((x * n_y + y) * 2 + c, ((y // 2) * n_y + 2 * x + y % 2) * 2 + c))
    return lax.ppermute(summed, ("x", "y", "c"), to)


def thirds(value):
    first = value.astype(jnp.bfloat16)
    rest = value - first.astype(jnp.float32)
    second = rest.astype(jnp.bfloat16)
    third = (rest - second.astype(jnp.float32)).astype(jnp.bfloat16)
    return first, second, third


def exact_dot(value, other, dims):
    dot = functools.partial(lax.dot_general, dimension_numbers=(dims, ((), ())), preferred_element_type=jnp.float32)
    count = value.shape[0]
    parts = dot(jnp.concatenate(thirds(value), axis=0), other)
    return (parts[2 * count :] + parts[count : 2 * count]) + parts[:count]


def mixed_kernel(basis, grads, out):
    mixed = exact_dot(basis[...], grads[...], ((1,), (1,)))
    few = out.shape[1]
    for t in range(out.shape[0]):
        out[t] = mixed[t * few : (t + 1) * few]


def left_kernel(arrived, activations, out, lines):
    few = arrived.shape[1]
    mixed = arrived[0]
    for t in range(1, arrived.shape[0]):
        mixed += arrived[t]
    for i, part in enumerate(thirds(mixed)):
        lines[i * few : (i + 1) * few] = part.astype(jnp.float32)
    dot = jnp.dot(lines[: 3 * few].astype(jnp.bfloat16), activations[...], preferred_element_type=jnp.float32)
    total = (dot[2 * few :] + dot[few : 2 * few]) + dot[:few]
    rows = out.shape[2]
    for d in range(out.shape[0]):
        out[d] = total[:, d * rows : (d + 1) * rows]


def seen_kernel(arrived, activations, mine, out, lines):
    n_d, few, rows = arrived.shape
    tokens = activations.shape[0]
    for d in range(n_d):
        lines[:few, d * rows : (d + 1) * rows] = arrived[d]
    left = lines[:few]
    for i, part in enumerate(thirds(left)):
        lines[i * few : (i + 1) * few] = part.astype(jnp.float32)
    dims = (((1,), (1,)), ((), ()))
    dot = lax.dot_general(
        lines[: 3 * few].astype(jnp.bfloat16), activations[...], dims, preferred_element_type=jnp.float32
    )
    seen = (dot[2 * few :] + dot[few : 2 * few]) + dot[:few]
    for t in range(out.shape[0]):
        out[t, :, :tokens] = seen
        out[t, :, tokens:] = mine[...]


def right_kernel(both, grads, out, left_rows, lines):
    tokens, hidden = grads.shape
    n_t, few, _ = both.shape
    rank = n_t * few
    for t in range(n_t):
        lines[t * few : (t + 1) * few] = both[t]
    right = exact_dot(lines[:, :tokens], grads[...], ((1,), (0,)))
    rows = lines[:, tokens:]
    left_rows[...] = rows
    gram = lax.dot_general(rows, rows, (((1,), (1,)), ((), ())), precision=HIGH, preferred_element_type=jnp.float32)
    few = out.shape[1]
    for d in range(out.shape[0]):
        out[d, :, :hidden] = right[d * few : (d + 1) * few]
        out[d, :, hidden : hidden + rank] = gram[d * few : (d + 1) * few]
        out[d, :, hidden + rank :] = jnp.zeros((few, out.shape[2] - hidden - rank), jnp.float32)


def spread_kernel(arrived, mine, out):
    total = arrived[0]
    for d in range(1, arrived.shape[0]):
        total += arrived[d]
    mine[...] = total
    for d in range(out.shape[0]):
        out[d] = total


def last_kernel(token_total, arrived, left_rows, weight, right_basis, new_weight, packed):
    few = arrived.shape[1]
    for d in range(arrived.shape[0]):
        packed[d * few : (d + 1) * few] = arrived[d]
    rank = packed.shape[0]
    hidden = weight.shape[1]
    row = lax.broadcasted_iota(jnp.int32, (8, 2 * rank), 0)
    lane = lax.broadcasted_iota(jnp.int32, (8, 2 * rank), 1)
    blocks = []
    for j in range(rank // 8):
        gram = packed[8 * j : 8 * j + 8, hidden : hidden + 2 * rank]
        blocks.append(jnp.where(lane < rank, gram, jnp.where(lane - rank == row + 8 * j, 1.0, 0.0)))
    for k in range(rank):
        b, i = divmod(k, 8)
        pivot = blocks[b][i : i + 1]
        scaled = pivot / pivot[:, k : k + 1]
        for j in range(b, rank // 8):
            factor = blocks[j][:, k : k + 1]
            if j == b:
                factor = jnp.where(row[:, :1] > i, factor, 0.0)
            blocks[j] = blocks[j] - factor * scaled
    inverse = []
    for j, block in enumerate(blocks):
        pivots = jnp.sum(jnp.where(lane == row + 8 * j, block, 0.0), axis=1, keepdims=True)
        inverse.append(block / jnp.sqrt(pivots))
    inverse = jnp.concatenate(inverse, axis=0)[:, rank:]
    dot = functools.partial(jnp.dot, precision=HIGH, preferred_element_type=jnp.float32)
    right = dot(inverse, packed[:, :hidden])
    basis = dot(inverse, left_rows[...])
    right_basis[...] = right / jnp.sqrt(jnp.float32(token_total))
    new_weight[...] = weight[...].astype(jnp.float32) - learn_rate * dot(basis.T, right)


def hold_kernel(source, out, done):
    copy = pltpu.make_async_copy(source, out, done)
    copy.start()
    copy.wait()


def hold(x):
    return pl.pallas_call(
        hold_kernel,
        out_shape=pltpu.VMEM(x.shape, x.dtype),
        in_specs=[pl.BlockSpec(memory_space=pl.ANY)],
        out_specs=pl.BlockSpec(memory_space=pltpu.VMEM),
        scratch_shapes=[pltpu.SemaphoreType.DMA],
        compiler_params=pltpu.CompilerParams(vmem_limit_bytes=4 << 20),
        name="hold",
    )(pltpu.with_memory_space_constraint(x, pltpu.HBM))


def run(kernel, shapes, *args, scratch=(), held=True, out=jax.ShapeDtypeStruct):
    vmem = pl.BlockSpec(memory_space=pltpu.VMEM)
    space = pltpu.VMEM if held else pltpu.HBM
    args = [pltpu.with_memory_space_constraint(a, space) for a in args]
    several = isinstance(shapes[0], tuple)
    outs = [out(s, jnp.float32) for s in (shapes if several else (shapes,))]
    return pl.pallas_call(
        kernel,
        out_shape=outs if several else outs[0],
        in_specs=[vmem] * len(args),
        out_specs=[vmem] * len(outs) if several else vmem,
        scratch_shapes=scratch,
        compiler_params=pltpu.CompilerParams(vmem_limit_bytes=12 << 20),
    )(*args)


def step(activations, grad_output, weight, start_basis):
    n_d, n_t = lax.axis_size(DP), lax.axis_size(TENSOR)
    tokens, features = activations.shape
    rows, hidden = weight.shape
    rank = start_basis.shape[1]
    few = rank // n_t
    f32 = jnp.float32
    input_grad = input_gradient(grad_output, weight)
    mixed = run(mixed_kernel, (n_t, few, tokens), start_basis.T, grad_output, held=False)
    activations = hold(activations)
    mixed = swap(mixed, TENSOR)
    left_part = run(left_kernel, (n_d, few, rows), mixed, activations, scratch=[pltpu.VMEM((16, tokens), f32)])
    left_mine = swap(left_part, DP)
    left_mine, left_few = run(spread_kernel, ((few, rows), (n_d, few, rows)), left_mine, out=pltpu.HBM)
    left_few = swap(left_few, DP)
    both = run(
        seen_kernel,
        (n_t, few, tokens + rows),
        left_few,
        activations,
        left_mine,
        scratch=[pltpu.VMEM((16, features), f32)],
    )
    both = swap(both, TENSOR)
    width = hidden + 128
    packed, left_rows = run(
        right_kernel,
        ((n_d, rank // n_d, width), (rank, rows)),
        both,
        grad_output,
        scratch=[pltpu.VMEM((rank, tokens + rows), f32)],
    )
    packed = swap(packed, DP)
    _, packed = run(spread_kernel, ((rank // n_d, width), (n_d, rank // n_d, width)), packed, out=pltpu.HBM)
    packed = swap(packed, DP)
    right_basis, new_weight = run(
        functools.partial(last_kernel, tokens * n_d),
        ((rank, hidden), (rows, hidden)),
        packed,
        left_rows,
        weight,
        scratch=[pltpu.VMEM((rank, width), f32)],
    )
    return (input_grad, right_basis.T, new_weight)


def solution(mesh):
    finer = Mesh(mesh.devices.reshape(4, 8, 8, 2), ("x", "z", "y", "c"))
    in_specs = (P(DP, None), P(DP, TENSOR), P(DP, TENSOR), P(TENSOR, None))
    out_specs = (P(DP, TENSOR), P(TENSOR, None), P(DP, TENSOR))
    return jax.shard_map(step, mesh=finer, in_specs=in_specs, out_specs=out_specs, check_vma=False)
```
